128 devices in a mesh: row: 8 (over z, x_hi), col: 16 (over x_lo, y, core).
Axes of the slice: x: 4 (x_hi: 2, x_lo: 2; x = x_hi * 2 + x_lo), y: 4, z: 4, core: 2. Of those that a mesh axis runs over, the one named last changes fastest.
Arguments:
- tiles: bfloat16 [8, 16, 32, 128, 128], P('row', 'col'), may hold values from 1.347065e-05 to 0.013427734
- tile_rows: int32 [8, 16, 32], P('row', 'col'), may hold values from 0 to 127, as said below
- tile_cols: int32 [8, 16, 32], P('row', 'col'), may hold values from 0 to 63, as said below
- start_vectors: float32 [64, 131072], P(None, ('row', 'col')), may hold values from -6 to 6
Outputs:
- ritz: float32 [64, 131072], P(None, ('row', 'col'))
- rayleigh: float32 [64, 64], replicated
The draws below stay inside these ranges and needn't reach their ends.
Inputs may be any that keep to these rules, and one draw needn't show every extreme that they name: `tile_rows`: tile row of each stored tile inside its block row; tile rows g * 8 to g * 8 + 7 belong to the block row's node group g. One block holds at most 4 tiles in the rows of any one node group, and exactly 4 in the rows of its own node group (group r * 16 + c of block r, c); in every block row one node group receives exactly 4 tiles from every block of that block row. The same position may repeat, and such tiles add. `tile_cols`: tile column of each stored tile inside its block column; tiles in the rows of the block's own node group lie in that group's columns.
All inputs are finite; a program needn't handle non-finite values.
Results may differ from the reference program's by a relative error of at most 0.00044.
Values may be sent and summed in bfloat16 or wider, within the bound.
A program may use at most 64 MiB of HBM per device.

```python
import math
import jax
import jax.numpy as jnp
from jax import lax

K = 64
TB = 128
TILES_PER_BLOCK = 32
CAP = 4
GROUP_TILES = 8
ROW_TILES = 128
COL_TILES = 64
NN = 131072
N_ROW = 8
N_COL = 16


def tile_pattern(key):
    slot_total_count = N_COL * CAP
    owning_blocks = jnp.arange(slot_total_count, dtype=jnp.int32) // CAP
    grid_rows = jnp.repeat(jnp.arange(N_ROW, dtype=jnp.int32), N_COL)
    grid_cols = jnp.tile(jnp.arange(N_COL, dtype=jnp.int32), N_ROW)

    def one_block(block_row, block_column_index):
        block_key = jax.random.fold_in(key, block_row * N_COL + block_column_index)
        central_node = jax.random.randint(jax.random.fold_in(key, 100003 + block_row), (), 0, N_COL)
        first, second, third, fourth = jax.random.split(block_key, 4)
        sorted_indices = jax.random.permutation(first, slot_total_count).astype(jnp.int32)
        extra_weight = jnp.where((owning_blocks == block_column_index) | (owning_blocks == central_node), slot_total_count, 0).astype(jnp.int32)
        selected_nodes = jnp.argsort(-(sorted_indices + extra_weight), stable=True)[:TILES_PER_BLOCK].astype(jnp.int32)
        owner = selected_nodes // CAP
        offset = jax.random.randint(second, (TILES_PER_BLOCK,), 0, GROUP_TILES).astype(jnp.int32)
        rows_out = owner * GROUP_TILES + offset
        nearby = (offset + jax.random.randint(third, (TILES_PER_BLOCK,), 0, 2).astype(jnp.int32)) % GROUP_TILES
        spread = jax.random.randint(fourth, (TILES_PER_BLOCK,), 0, COL_TILES).astype(jnp.int32)
        cols_out = jnp.where(owner == block_column_index, block_row * GROUP_TILES + nearby, spread)
        return (rows_out, cols_out)
    rows_all, cols_all = jax.vmap(one_block)(grid_rows, grid_cols)
    return (rows_all.reshape(N_ROW, N_COL, TILES_PER_BLOCK).astype(jnp.int32), cols_all.reshape(N_ROW, N_COL, TILES_PER_BLOCK).astype(jnp.int32))


def draw_tile_rows(key, part):
    return tile_pattern(jax.random.fold_in(key, 4242))[0]


def draw_tile_cols(key, part):
    return tile_pattern(jax.random.fold_in(key, 4242))[1]


def levels(own_key, dims, shards, low, high):
    gain = 1.0
    for position, shards_of in shards:
        heights = jax.random.uniform(jax.random.fold_in(jax.random.fold_in(own_key, 6), position), (shards_of,), jnp.float32, low / len(shards), high / len(shards))
        gain = gain * jnp.repeat(jnp.exp(heights), dims[position] // shards_of).reshape((-1,) + (1,) * (len(dims) - 1 - position))
    return gain


def normal_values(rng, extent, scale, bound, cuts=(), kind=jnp.bfloat16):
    level = levels(rng, extent, cuts, -0.22, 0.18) if cuts else 1.0
    values = jax.random.normal(rng, extent, jnp.float32) * scale * level
    return jnp.minimum(jnp.maximum(values, -bound), bound).astype(kind)


def setup_inputs(seed: int = 0) -> dict:
    streams_of = jax.random.split(jax.random.key(seed), 5)
    tiles = jnp.clip(jnp.exp(math.log(0.013427734) - 6.9045644 * jax.random.uniform(streams_of[0], (N_ROW, N_COL, TILES_PER_BLOCK, TB, TB), jnp.float32) ** levels(streams_of[0], (N_ROW, N_COL, TILES_PER_BLOCK, TB, TB), ((0, 8), (1, 16)), -0.2, 0.2)), 1.3470649719238281e-05, 0.013427734).astype(jnp.bfloat16)
    tile_rows = draw_tile_rows(jax.random.fold_in(streams_of[4], 71), 0)
    tile_cols = draw_tile_cols(jax.random.fold_in(streams_of[4], 71), 0)
    start_vectors = normal_values(streams_of[3], (K, NN), 1.0, 6.0, ((1, 128),), jnp.float32)
    return {"tiles": tiles, "tile_rows": tile_rows, "tile_cols": tile_cols, "start_vectors": start_vectors}


CENTER = 1.0
HALF_WIDTH = 0.5

def tile_index(tile_rows, tile_cols):
    block_row = jnp.arange(N_ROW, dtype=jnp.int32)[:, None, None]
    block_column_index = jnp.arange(N_COL, dtype=jnp.int32)[None, :, None]
    row_index = block_row * ROW_TILES + tile_rows
    col_index = tile_cols // GROUP_TILES * (N_COL * GROUP_TILES) + block_column_index * GROUP_TILES + tile_cols % GROUP_TILES
    return (row_index.reshape(N_ROW * N_COL, TILES_PER_BLOCK).astype(jnp.int32), col_index.reshape(N_ROW * N_COL, TILES_PER_BLOCK).astype(jnp.int32))

def node_degree(blocks, row_index, col_index):

    def visit(totals, device):
        row_total, col_total = totals
        tile_float = blocks[device].astype(jnp.float32)
        row_total = row_total.at[row_index[device]].add(jnp.sum(tile_float, axis=2))
        col_total = col_total.at[col_index[device]].add(jnp.sum(tile_float, axis=1))
        return ((row_total, col_total), None)
    start = (jnp.zeros((NN // TB, TB), jnp.float32), jnp.zeros((NN // TB, TB), jnp.float32))
    (row_total, col_total), _ = lax.scan(visit, start, jnp.arange(N_ROW * N_COL, dtype=jnp.int32))
    return 0.5 * (row_total + col_total).reshape(NN)

def symmetric_part(vectors, blocks, row_index, col_index):
    rounded = lax.optimization_barrier(vectors.astype(jnp.bfloat16)).astype(jnp.float32)
    rounded = rounded.reshape(K, NN // TB, TB)

    def visit(totals, device):
        row_total, col_total = totals
        tile_float = blocks[device].astype(jnp.float32)
        picked_cols = jnp.take(rounded, col_index[device], axis=1)
        picked_rows = jnp.take(rounded, row_index[device], axis=1)
        row_term = jnp.einsum('tij,ktj->kti', tile_float, picked_cols)
        col_term = jnp.einsum('tij,kti->ktj', tile_float, picked_rows)
        row_total = row_total.at[:, row_index[device]].add(row_term)
        col_total = col_total.at[:, col_index[device]].add(col_term)
        return ((row_total, col_total), None)
    start = (jnp.zeros((K, NN // TB, TB), jnp.float32), jnp.zeros((K, NN // TB, TB), jnp.float32))
    (row_total, col_total), _ = lax.scan(visit, start, jnp.arange(N_ROW * N_COL, dtype=jnp.int32))
    return 0.5 * (row_total + col_total).reshape(K, NN)

def reference(tiles, tile_rows, tile_cols, start_vectors):
    blocks = tiles.reshape(N_ROW * N_COL, TILES_PER_BLOCK, TB, TB)
    row_index, col_index = tile_index(tile_rows, tile_cols)
    degree = node_degree(blocks, row_index, col_index)
    highest = lax.Precision.HIGHEST

    def laplace(vectors):
        return degree[None, :] * vectors - symmetric_part(vectors, blocks, row_index, col_index)
    first_step = (laplace(start_vectors) - CENTER * start_vectors) / HALF_WIDTH
    filtered = 2.0 * (laplace(first_step) - CENTER * first_step) / HALF_WIDTH - start_vectors
    gram_matrix = jnp.dot(filtered, filtered.T, precision=highest) / NN
    factor = jnp.linalg.cholesky(gram_matrix)
    inverse = jax.scipy.linalg.solve_triangular(factor, jnp.eye(K, dtype=jnp.float32), lower=True)
    block = jnp.dot(inverse, filtered, precision=highest)
    image = laplace(block)
    rayleigh = jnp.dot(block, image.T, precision=highest) / NN
    ritz = jnp.dot(rayleigh.T, block, precision=highest)
    return (ritz, rayleigh)
```

```python
import functools

import jax
import jax.numpy as jnp
from jax import lax
from jax.experimental import pallas as pl
from jax.experimental.pallas import tpu as pltpu
from jax.sharding import PartitionSpec as P

MESH = pl.DeviceIdType.MESH
F32, BF16, I16 = jnp.float32, jnp.bfloat16, jnp.int16
HIGH = lax.Precision.HIGHEST
CENTER = 1.0
HALF_WIDTH = 0.5
K = 64
TB = 128
NT = 32
CAP = 4
GT = 8
N_ROW, N_COL = 8, 16
NN = 131072
COLS, ROWS, PREV, LAST, SLOT, RID = 0, 32, 64, 96, 160, 224
TAB = 288
NSEM = 192
STEPS = 32767.0


def table_kernel(rows_ref, cols_ref, tab, count):
    def clear(i, _):
        tab[LAST + i] = NT
        tab[SLOT + i] = NT
        tab[RID + i] = -1
        return 0

    lax.fori_loop(0, 64, clear, 0)
    for g in range(N_COL):
        count[g] = 0

    def put(t, _):
        r, c = rows_ref[t], cols_ref[t]
        tab[COLS + t] = c
        tab[ROWS + t] = r
        g = r // GT
        s = count[g]
        count[g] = s + 1
        tab[SLOT + g * CAP + s] = t
        tab[RID + g * CAP + s] = r % GT
        tab[PREV + t] = tab[LAST + c]
        tab[LAST + c] = t
        return 0

    lax.fori_loop(0, NT, put, 0)


def dot_t(a, b, **kw):
    return lax.dot_general(a, b, (((1,), (1,)), ((), ())), preferred_element_type=F32, **kw)


def dot_n(a, b, **kw):
    return lax.dot_general(a, b, (((1,), (0,)), ((), ())), preferred_element_type=F32, **kw)


def spread(x):
    m = jnp.max(jnp.max(x, axis=0, keepdims=True), axis=1, keepdims=True)
    return jnp.broadcast_to(jnp.maximum(m, 1e-30), x.shape)


def largest(x):
    return jnp.max(jnp.abs(x).reshape(-1, 8, TB), axis=0)


def code(x, rate):
    return jnp.round(x * rate).astype(jnp.int32).astype(I16)


def plain(x):
    return x.astype(jnp.int32).astype(F32)


def main_kernel(
    tab, tiles, v_ref, f_ref, g_ref,
    colp, rowp, prod, chain, srow, rrow, scol, rcol, sxl, rxl, sxh, rxh, arow, acol,
    rsum, csum, srd, rrd, scd, rcd, sxld, rxld, sxhd, rxhd, deg, mk, f1,
    a_in, a_r, b_r, c_r, unit, runit, zunit, xlu, rxlu, xhu, rxhu, ssem, rsem,
):
    row, col = lax.axis_index("row"), lax.axis_index("col")
    z, xh = row // 2, row % 2
    xl, j = col // 8, col % 8
    y, c = j // 2, j % 2
    oxl, oxh = 1 - xl, 1 - xh

    def col_dev(xl_, j_):
        return (row, xl_ * 8 + j_)

    def row_dev(z_, xh_):
        return (z_ * 2 + xh_, col)

    barrier = pltpu.get_barrier_semaphore()
    for d in range(1, N_ROW):
        pl.semaphore_signal(barrier, inc=1, device_id=((row + d) % N_ROW, col), device_id_type=MESH)
    for d in range(1, N_COL):
        pl.semaphore_signal(barrier, inc=1, device_id=(row, (col + d) % N_COL), device_id_type=MESH)

    sent = []

    def send(src, dst, dev):
        k = len(sent)
        copy = pltpu.make_async_remote_copy(
            src_ref=src, dst_ref=dst, send_sem=ssem.at[k], recv_sem=rsem.at[k],
            device_id=dev, device_id_type=MESH,
        )
        sent.append(copy)
        copy.start()
        return copy

    def own_block(p, value_of):
        for q in range(GT):
            b = value_of(q).astype(BF16)
            colp[p, row * GT + q] = b
            rowp[p, col * GT + q] = b

    def gather_start(p):
        def crow(r_):
            return colp.at[p, pl.ds(r_ * GT, GT)]

        def rcol_(c_):
            return rowp.at[p, pl.ds(c_ * GT, GT)]

        x1 = send(rcol_(col), rcol_(col), col_dev(oxl, j))
        x2 = send(crow(row), crow(row), row_dev(z, oxh))
        ys, zs = [], []
        for d in (1, 3, 2):
            ys.append((d, send(rcol_(col), rcol_(col), col_dev(xl, (y + d) % 4 * 2 + c))))
            zs.append((d, send(crow(row), crow(row), row_dev((z + d) % 4, xh))))
        c0 = send(rcol_(col), rcol_(col), col_dev(xl, y * 2 + 1 - c))
        return crow, rcol_, x1, x2, ys, zs, [c0]

    def gather_end(state):
        crow, rcol_, x1, x2, ys, zs, cs = state

        def core(b):
            cs.append(send(rcol_(b), rcol_(b), col_dev(xl, y * 2 + 1 - c)))

        x1.wait_recv()
        b = oxl * 8 + j
        yf = [(d, send(rcol_(b), rcol_(b), col_dev(xl, (y + d) % 4 * 2 + c))) for d in (1, 3, 2)]
        core(b)
        x2.wait_recv()
        b = z * 2 + oxh
        zf = [send(crow(b), crow(b), row_dev((z + d) % 4, xh)) for d in (1, 3, 2)]
        for d, copy in ys:
            copy.wait_recv()
            core(xl * 8 + (y + 4 - d) % 4 * 2 + c)
        for _, copy in zs:
            copy.wait_recv()
        for d, copy in yf:
            copy.wait_recv()
            core(oxl * 8 + (y + 4 - d) % 4 * 2 + c)
        for copy in zf + cs:
            copy.wait_recv()

    def degree_start():
        ones = jnp.ones((16, TB), BF16)
        rsum[NT] = jnp.zeros((8, TB), F32)
        csum[NT] = jnp.zeros((8, TB), F32)

        def body(i, _):
            sums = []
            for u in range(4):
                tile = tiles[i * 4 + u]
                sums.append((dot_t(ones, tile), dot_n(ones, tile)))
            for u in range(4):
                t = i * 4 + u
                rsum[t] = sums[u][0][:8]
                csum[t] = sums[u][1][:8] + csum[tab[PREV + t]]
            return 0

        lax.fori_loop(0, NT // 4, body, 0)

        def row_body(jj, _):
            for x in range(2):
                for s in range(CAP):
                    slot = (x * 8 + jj) * CAP + s
                    i = x * CAP + s
                    srd[jj, i : i + 1] = rsum[tab[SLOT + slot]][0:1]
                    srd[jj, 8 + i : 9 + i] = jnp.full((1, TB), tab[RID + slot].astype(F32))
            return 0

        lax.fori_loop(0, 8, row_body, 0)

        def col_body(i, _):
            for x in range(2):
                for q in range(GT):
                    n = x * GT + q
                    scd[i, n : n + 1] = csum[tab[LAST + (i * 2 + x) * GT + q]][0:1]
            return 0

        lax.fori_loop(0, 4, col_body, 0)
        out = []
        for d in range(1, 8):
            j_ = (y + d // 2) % 4 * 2 + (c + d) % 2
            out.append(send(srd.at[j_], rrd.at[j], col_dev(xl, j_)))
        for d in (1, 3, 2):
            out.append(send(scd.at[(z + d) % 4], rcd.at[z], row_dev((z + d) % 4, xh)))
        rrd[j] = srd[j]
        rcd[z] = scd[z]
        return out

    def degree_middle(copies):
        for copy in copies:
            copy.wait_recv()
        lane = lax.broadcasted_iota(jnp.int32, (8, TB), 0).astype(F32)

        def masks(jj, _):
            for x in range(2):
                for s in range(CAP):
                    i = 8 + x * CAP + s
                    rid = jnp.broadcast_to(rrd[jj, i : i + 1], (8, TB))
                    for q in range(GT):
                        mk[x, jj, s, q] = jnp.where(rid == float(q), 1.0, 0.0)
            return 0

        lax.fori_loop(0, 8, masks, 0)

        def total(x):
            acc = jnp.zeros((8, TB), F32)
            for jj in range(8):
                for s in range(CAP):
                    val = rrd[jj, pl.ds(x * CAP + s, 1)]
                    rid = rrd[jj, pl.ds(8 + x * CAP + s, 1)]
                    acc = acc + jnp.where(rid == lane, val, 0.0)
            return acc

        first, second = total(0), total(1)
        mine = jnp.where(xl == 0, first, second)
        sxld[...] = jnp.where(xl == 0, second, first)
        s1 = send(sxld, rxld, col_dev(oxl, j))

        def csum_of(x):
            return sum(rcd[zz, x * 8 : x * 8 + 8] for zz in range(4))

        first, second = csum_of(0), csum_of(1)
        cmine = jnp.where(xh == 0, first, second)
        sxhd[...] = jnp.where(xh == 0, second, first)
        s2 = send(sxhd, rxhd, row_dev(z, oxh))
        deg[...] = mine + cmine
        return s1, s2

    def degree_end(copies):
        for copy in copies:
            copy.wait_recv()
        deg[...] = 0.5 * (deg[...] + rxld[...] + rxhd[...])

    def products(p):
        def body(i, top):
            out = []
            for u in range(4):
                t = i * 4 + u
                tile = tiles[t]
                out.append((dot_t(colp[p, tab[COLS + t]], tile), dot_n(rowp[p, tab[ROWS + t]], tile)))
            for u in range(4):
                t = i * 4 + u
                prod[t] = out[u][0]
                total = out[u][1] + chain[tab[PREV + t]]
                chain[t] = total
                top = jnp.maximum(top, jnp.maximum(largest(out[u][0]), largest(total)))
            return top

        return lax.fori_loop(0, NT // 4, body, jnp.zeros((8, TB), F32))

    def scatter_sums(p, top):
        top = spread(top)
        rate = (STEPS / top)[:1]
        unit[p] = top * (1.0 / STEPS)
        runit[p, j] = unit[p]
        zunit[p, z] = unit[p]
        ucopies = []
        for d in range(1, 8):
            j_ = (y + d // 2) % 4 * 2 + (c + d) % 2
            ucopies.append(send(unit.at[p], runit.at[p, j], col_dev(xl, j_)))
        for d in (1, 3, 2):
            ucopies.append(send(unit.at[p], zunit.at[p, z], row_dev((z + d) % 4, xh)))

        def row_body(jj, _):
            for x in range(2):
                for s in range(CAP):
                    srow[p, jj, x, s] = code(prod[tab[SLOT + (x * 8 + jj) * CAP + s]], rate)
            return 0

        lax.fori_loop(0, 8, row_body, 0)
        rcopies = []
        for d in range(1, 8):
            j_ = (y + d // 2) % 4 * 2 + (c + d) % 2
            rcopies.append(send(srow.at[p, j_], rrow.at[p, j], col_dev(xl, j_)))

        def col_body(i, _):
            for x in range(2):
                for q in range(GT):
                    scol[p, i, x, q] = code(chain[tab[LAST + (i * 2 + x) * GT + q]], rate)
            return 0

        lax.fori_loop(0, 4, col_body, 0)
        ccopies = []
        for d in (1, 3, 2):
            ccopies.append(send(scol.at[p, (z + d) % 4], rcol.at[p, z], row_dev((z + d) % 4, xh)))
        rrow[p, j] = srow[p, j]
        rcol[p, z] = scol[p, z]
        for copy in ucopies + ccopies:
            copy.wait_recv()

        def col_sum(x, q):
            total = plain(rcol[p, 0, x, q]) * zunit[p, 0, 0:1]
            for zz in range(1, 4):
                total = total + plain(rcol[p, zz, x, q]) * zunit[p, zz, 0:1]
            return total

        def other_col(q, top):
            total = col_sum(oxh, q)
            acol[q] = total
            return jnp.maximum(top, largest(total))

        top = spread(lax.fori_loop(0, GT, other_col, jnp.zeros((8, TB), F32)))
        xhu[p] = top * (1.0 / STEPS)
        u2 = send(xhu.at[p], rxhu.at[p], row_dev(z, oxh))
        rate = (STEPS / top)[:1]

        def code_col(q, _):
            sxh[p, q] = code(acol[q], rate)
            return 0

        lax.fori_loop(0, GT, code_col, 0)
        s2 = send(sxh.at[p], rxh.at[p], row_dev(z, oxh))

        def own_col(q, _):
            acol[q] = col_sum(xh, q)
            return 0

        lax.fori_loop(0, GT, own_col, 0)
        for copy in rcopies:
            copy.wait_recv()

        def row_sum(x):
            def chunk(kc, top):
                rows = pl.ds(pl.multiple_of(kc * 16, 16), 16)

                def source(jj, accs):
                    accs = list(accs)
                    factor = runit[p, jj]
                    for s in range(CAP):
                        data = (plain(rrow[p, jj, x, s, rows])).reshape(2, 8, TB) * factor[None]
                        for q in range(GT):
                            accs[q] = accs[q] + data * mk[x, jj, s, q][None]
                    return tuple(accs)

                accs = lax.fori_loop(
                    0, 8, source, tuple(jnp.zeros((2, 8, TB), F32) for _ in range(GT))
                )
                for q in range(GT):
                    value = accs[q].reshape(16, TB)
                    arow[q, rows] = value
                    top = jnp.maximum(top, largest(value))
                return top

            return lax.fori_loop(0, K // 16, chunk, jnp.zeros((8, TB), F32))

        top = spread(row_sum(oxl))
        xlu[p] = top * (1.0 / STEPS)
        u1 = send(xlu.at[p], rxlu.at[p], col_dev(oxl, j))
        rate = (STEPS / top)[:1]

        def code_row(q, _):
            sxl[p, q] = code(arow[q], rate)
            return 0

        lax.fori_loop(0, GT, code_row, 0)
        s1 = send(sxl.at[p], rxl.at[p], col_dev(oxl, j))
        row_sum(xl)
        for copy in (u2, s2, u1, s1):
            copy.wait_recv()

    def symmetric(p, q):
        total = arow[q] + acol[q]
        total = total + plain(rxl[p, q]) * rxlu[p, 0:1] + plain(rxh[p, q]) * rxhu[p, 0:1]
        return 0.5 * total

    def lanes(q):
        return slice(q * TB, (q + 1) * TB)

    own_block(0, lambda q: v_ref[:, lanes(q)])
    prod[NT] = jnp.zeros((K, TB), F32)
    chain[NT] = jnp.zeros((K, TB), F32)
    pl.semaphore_wait(barrier, N_ROW - 1 + N_COL - 1)
    state = gather_start(0)
    dcopies = degree_start()
    gather_end(state)
    top = products(0)
    dlast = degree_middle(dcopies)
    scatter_sums(0, top)
    degree_end(dlast)
    for q in range(GT):
        v = v_ref[:, lanes(q)]
        image = deg[q : q + 1] * v - symmetric(0, q)
        f1[:, lanes(q)] = (image - CENTER * v) / HALF_WIDTH
    own_block(1, lambda q: f1[:, lanes(q)])
    gather_end(gather_start(1))
    scatter_sums(1, products(1))
    for q in range(GT):
        v = f1[:, lanes(q)]
        image = deg[q : q + 1] * v - symmetric(1, q)
        f_ref[:, lanes(q)] = 2.0 * (image - CENTER * v) / HALF_WIDTH - v_ref[:, lanes(q)]
    own_block(2, lambda q: f_ref[:, lanes(q)])
    state = gather_start(2)
    gram = jnp.zeros((K, K), F32)
    diag = jnp.zeros((K, K), F32)
    for q in range(GT):
        f = f_ref[:, lanes(q)]
        gram = gram + dot_t(f, f, precision=HIGH)
        diag = diag + dot_t(f, deg[q : q + 1] * f, precision=HIGH)
    gather_end(state)

    def form(i, acc):
        parts = []
        for u in range(4):
            t = i * 4 + u
            parts.append(dot_t(colp[2, tab[COLS + t]], tiles[t]).astype(BF16))
        for u in range(4):
            acc = acc + dot_t(parts[u], rowp[2, tab[ROWS + i * 4 + u]])
        return acc

    form_w = lax.fori_loop(0, NT // 4, form, jnp.zeros((K, K), F32))
    both = jnp.concatenate([gram, diag - form_w], axis=1)
    for r in range(N_ROW):
        a_in[r] = both[r * 8 : r * 8 + 8]
    copies = []
    for d in range(1, N_ROW):
        r_ = (row + d) % N_ROW
        copies.append(send(a_in.at[r_], a_r.at[row], (r_, col)))
    a_r[row] = a_in[row]
    for copy in copies:
        copy.wait_recv()
    total = a_r[0]
    for r in range(1, N_ROW):
        total = total + a_r[r]
    b_r[col] = total
    copies = []
    for d in range(1, N_COL):
        copies.append(send(b_r.at[col], b_r.at[col], (row, (col + d) % N_COL)))
    for copy in copies:
        copy.wait_recv()
    total = b_r[0]
    for r in range(1, N_COL):
        total = total + b_r[r]
    c_r[row] = total
    copies = []
    for d in range(1, N_ROW):
        copies.append(send(c_r.at[row], c_r.at[row], ((row + d) % N_ROW, col)))
    for copy in copies:
        copy.wait_recv()
    for r in range(N_ROW):
        g_ref[r * 8 : r * 8 + 8] = c_r[r]
    for copy in sent:
        copy.wait_send()


def final_kernel(g_ref, f_ref, ritz_ref, ray_ref):
    both = g_ref[...] * (1.0 / NN)
    sub = lax.broadcasted_iota(jnp.int32, (K, 2 * K), 0)
    lane = lax.broadcasted_iota(jnp.int32, (K, 2 * K), 1)
    left = lane < K
    eye = jnp.where(lane == sub + K, 1.0, 0.0)
    a = jnp.where(left, both, eye)
    for i in range(K):
        inv = 1.0 / jnp.sqrt(a[i : i + 1, i : i + 1])
        pivot = a[i : i + 1] * inv
        column = jnp.where(sub[:, :1] > i, a[:, i : i + 1] * inv, 0.0)
        a = jnp.where(sub == i, pivot, a - column * pivot)
    inverse = a[:, K:]
    q = both[:, K:]
    half = dot_n(inverse, q, precision=HIGH)
    ray = 0.5 * (dot_t(half, inverse, precision=HIGH) + dot_t(inverse, half, precision=HIGH))
    ray_ref[...] = ray
    ritz_ref[...] = dot_n(dot_n(ray, inverse, precision=HIGH), f_ref[...], precision=HIGH)


def local(tiles, tile_rows, tile_cols, start_vectors):
    smem = pl.BlockSpec(memory_space=pltpu.SMEM)
    vmem = pl.BlockSpec(memory_space=pltpu.VMEM)
    table = pl.pallas_call(
        table_kernel,
        out_shape=jax.ShapeDtypeStruct((TAB,), jnp.int32),
        in_specs=[smem, smem],
        out_specs=smem,
        scratch_shapes=[pltpu.SMEM((N_COL,), jnp.int32)],
    )(tile_rows.reshape(NT), tile_cols.reshape(NT))
    own = start_vectors.shape[1]
    V = pltpu.VMEM
    filtered, sums = pl.pallas_call(
        main_kernel,
        out_shape=(
            jax.ShapeDtypeStruct((K, own), F32),
            jax.ShapeDtypeStruct((K, 2 * K), F32),
        ),
        in_specs=[smem, vmem, vmem],
        out_specs=(vmem, vmem),
        scratch_shapes=[
            V((3, 64, K, TB), BF16), V((3, 128, K, TB), BF16),
            V((NT + 1, K, TB), F32), V((NT + 1, K, TB), F32),
            V((2, 8, 2, CAP, K, TB), I16), V((2, 8, 2, CAP, K, TB), I16),
            V((2, 4, 2, GT, K, TB), I16), V((2, 4, 2, GT, K, TB), I16),
            V((2, GT, K, TB), I16), V((2, GT, K, TB), I16),
            V((2, GT, K, TB), I16), V((2, GT, K, TB), I16),
            V((GT, K, TB), F32), V((GT, K, TB), F32),
            V((NT + 1, 8, TB), F32), V((NT + 1, 8, TB), F32),
            V((8, 16, TB), F32), V((8, 16, TB), F32),
            V((4, 16, TB), F32), V((4, 16, TB), F32),
            V((8, TB), F32), V((8, TB), F32), V((8, TB), F32), V((8, TB), F32),
            V((8, TB), F32), V((2, 8, CAP, GT, 8, TB), F32), V((K, own), F32),
            V((8, 8, TB), F32), V((8, 8, TB), F32), V((16, 8, TB), F32), V((8, 8, TB), F32),
            V((2, 8, TB), F32), V((2, 8, 8, TB), F32), V((2, 4, 8, TB), F32),
            V((2, 8, TB), F32), V((2, 8, TB), F32), V((2, 8, TB), F32), V((2, 8, TB), F32),
            pltpu.SemaphoreType.DMA((NSEM,)), pltpu.SemaphoreType.DMA((NSEM,)),
        ],
        compiler_params=pltpu.CompilerParams(
            collective_id=0, has_side_effects=True, vmem_limit_bytes=48 * 1024 * 1024
        ),
    )(table, tiles.reshape(NT, TB, TB), start_vectors)
    return pl.pallas_call(
        final_kernel,
        out_shape=(
            jax.ShapeDtypeStruct((K, own), F32),
            jax.ShapeDtypeStruct((K, K), F32),
        ),
        in_specs=[vmem, vmem],
        out_specs=(vmem, vmem),
    )(sums, filtered)


def solution(mesh):
    placed = (
        P("row", "col", None, None, None),
        P("row", "col", None),
        P("row", "col", None),
        P(None, ("row", "col")),
    )
    return jax.shard_map(
        local, mesh=mesh, in_specs=placed, out_specs=(P(None, ("row", "col")), P()), check_vma=False
    )
```

```python
import functools

import jax
import jax.numpy as jnp
from jax import lax
from jax.experimental import pallas as pl
from jax.experimental.pallas import tpu as pltpu
from jax.sharding import PartitionSpec as P

MESH = pl.DeviceIdType.MESH
F32, BF16, I16 = jnp.float32, jnp.bfloat16, jnp.int16
HIGH = lax.Precision.HIGHEST
CENTER = 1.0
HALF_WIDTH = 0.5
K = 64
TB = 128
NT = 32
CAP = 4
GT = 8
N_ROW, N_COL = 8, 16
NN = 131072
COLS, ROWS, PREV, LAST, SLOT, RID = 0, 32, 64, 96, 160, 224
TAB = 288
NH = 2
KH = K // NH
PH = 3 * NH
NSEM = 360
STEPS = 32767.0


def table_kernel(rows_ref, cols_ref, tab, count):
    def clear(i, _):
        tab[LAST + i] = NT
        tab[SLOT + i] = NT
        tab[RID + i] = -1
        return 0

    lax.fori_loop(0, 64, clear, 0)
    for g in range(N_COL):
        count[g] = 0

    def put(t, _):
        r, c = rows_ref[t], cols_ref[t]
        tab[COLS + t] = c
        tab[ROWS + t] = r
        g = r // GT
        s = count[g]
        count[g] = s + 1
        tab[SLOT + g * CAP + s] = t
        tab[RID + g * CAP + s] = r % GT
        tab[PREV + t] = tab[LAST + c]
        tab[LAST + c] = t
        return 0

    lax.fori_loop(0, NT, put, 0)


def dot_t(a, b, **kw):
    return lax.dot_general(a, b, (((1,), (1,)), ((), ())), preferred_element_type=F32, **kw)


def dot_n(a, b, **kw):
    return lax.dot_general(a, b, (((1,), (0,)), ((), ())), preferred_element_type=F32, **kw)


def spread(x):
    m = jnp.max(jnp.max(x, axis=0, keepdims=True), axis=1, keepdims=True)
    return jnp.broadcast_to(jnp.maximum(m, 1e-30), x.shape)


def largest(x):
    return jnp.max(jnp.abs(x).reshape(-1, 8, TB), axis=0)


def code(x, rate):
    return jnp.round(x * rate).astype(jnp.int32).astype(I16)


def plain(x):
    return x.astype(jnp.int32).astype(F32)


def main_kernel(
    tab, tiles_hbm, v_ref, ritz_ref, ray_ref,
    tiles, colp, rowp, prod, chain, srow, rrow, scol, rcol, sxl, rxl, sxh, rxh, arow, acol,
    rsum, csum, srd, rrd, scd, rcd, sxld, rxld, sxhd, rxhd, deg, mk, f1, f_ref,
    sum_a, sum_b, unit, runit, zunit, xlu, rxlu, xhu, rxhu, ssem, rsem, lsem,
):
    row, col = lax.axis_index("row"), lax.axis_index("col")
    z, xh = row // 2, row % 2
    xl, j = col // 8, col % 8
    y, c = j // 2, j % 2
    oxl, oxh = 1 - xl, 1 - xh

    def col_dev(xl_, j_):
        return (row, xl_ * 8 + j_)

    def row_dev(z_, xh_):
        return (z_ * 2 + xh_, col)

    barrier = pltpu.get_barrier_semaphore()
    for d in range(1, N_ROW):
        pl.semaphore_signal(barrier, inc=1, device_id=((row + d) % N_ROW, col), device_id_type=MESH)
    for d in range(1, N_COL):
        pl.semaphore_signal(barrier, inc=1, device_id=(row, (col + d) % N_COL), device_id_type=MESH)
    load = pltpu.make_async_copy(tiles_hbm, tiles, lsem)
    load.start()

    sent = []

    def send(src, dst, dev):
        k = len(sent)
        copy = pltpu.make_async_remote_copy(
            src_ref=src, dst_ref=dst, send_sem=ssem.at[k], recv_sem=rsem.at[k],
            device_id=dev, device_id_type=MESH,
        )
        sent.append(copy)
        copy.start()
        return copy

    def lanes(q):
        return slice(q * TB, (q + 1) * TB)

    def vecs(h):
        return slice(h * KH, (h + 1) * KH)

    class Gather:
        def __init__(self, ph, value_of):
            self.ph, self.cores = ph, []
            self.way, self.back = ((1, 3), (3, 1))[ph % 2]
            for q in range(GT):
                b = value_of(q).astype(BF16)
                colp[ph][row * GT + q] = b
                rowp[ph][col * GT + q] = b
            self.x1 = self.to_col(col, oxl, y, c)
            self.x2 = self.to_row(row, z, oxh)
            self.ys = [self.to_col(col, xl, (y + d) % 4, c) for d in (self.way, self.back)]
            self.zs = [self.to_row(row, (z + d) % 4, xh) for d in (self.way, self.back)]
            self.core(col)

        def to_col(self, b, xl_, y_, c_):
            ref = rowp[self.ph].at[pl.ds(b * GT, GT)]
            return send(ref, ref, col_dev(xl_, y_ * 2 + c_))

        def to_row(self, b, z_, xh_):
            ref = colp[self.ph].at[pl.ds(b * GT, GT)]
            return send(ref, ref, row_dev(z_, xh_))

        def core(self, b):
            self.cores.append(self.to_col(b, xl, y, 1 - c))

        def across(self):
            self.x1.wait_recv()
            b = oxl * 8 + j
            self.yf = [self.to_col(b, xl, (y + d) % 4, c) for d in (self.way, self.back)]
            self.core(b)
            self.x2.wait_recv()
            b = z * 2 + oxh
            self.zf = [self.to_row(b, (z + d) % 4, xh) for d in (self.way, self.back)]

        def relay(self):
            ahead = (y + self.way) % 4
            behind = (y + 4 - self.way) % 4
            zahead, zbehind = (z + self.way) % 4, (z + 4 - self.way) % 4
            self.far = []
            for x, ycopies, zx, zcopies in ((xl, self.ys, xh, self.zs), (oxl, self.yf, oxh, self.zf)):
                ycopies[0].wait_recv()
                b = x * 8 + behind * 2 + c
                yfar = self.to_col(b, xl, ahead, c)
                zcopies[0].wait_recv()
                zfar = self.to_row(zbehind * 2 + zx, zahead, xh)
                self.core(b)
                ycopies[1].wait_recv()
                self.core(x * 8 + ahead * 2 + c)
                self.far.append((x, yfar, zcopies[1], zfar))

        def end(self):
            for x, yfar, znear, zfar in self.far:
                yfar.wait_recv()
                self.core(x * 8 + (y + 2) % 4 * 2 + c)
            for x, yfar, znear, zfar in self.far:
                znear.wait_recv()
                zfar.wait_recv()
            for copy in self.cores:
                copy.wait_recv()

    def degree_start():
        ones = jnp.ones((16, TB), BF16)
        rsum[NT] = jnp.zeros((8, TB), F32)
        csum[NT] = jnp.zeros((8, TB), F32)

        def body(i, _):
            sums = []
            for u in range(4):
                tile = tiles[i * 4 + u]
                sums.append((dot_t(ones, tile), dot_n(ones, tile)))
            for u in range(4):
                t = i * 4 + u
                rsum[t] = sums[u][0][:8]
                csum[t] = sums[u][1][:8] + csum[tab[PREV + t]]
            return 0

        lax.fori_loop(0, NT // 4, body, 0)

        def row_body(jj, _):
            for x in range(2):
                for s in range(CAP):
                    slot = (x * 8 + jj) * CAP + s
                    i = x * CAP + s
                    srd[jj, i : i + 1] = rsum[tab[SLOT + slot]][0:1]
                    srd[jj, 8 + i : 9 + i] = jnp.full((1, TB), tab[RID + slot].astype(F32))
            return 0

        lax.fori_loop(0, 8, row_body, 0)

        def col_body(i, _):
            for x in range(2):
                for q in range(GT):
                    n = x * GT + q
                    scd[i, n : n + 1] = csum[tab[LAST + (i * 2 + x) * GT + q]][0:1]
            return 0

        lax.fori_loop(0, 4, col_body, 0)
        out = []
        for d in range(1, 8):
            j_ = (y + d // 2) % 4 * 2 + (c + d) % 2
            out.append(send(srd.at[j_], rrd.at[j], col_dev(xl, j_)))
        for d in (1, 3, 2):
            out.append(send(scd.at[(z + d) % 4], rcd.at[z], row_dev((z + d) % 4, xh)))
        rrd[j] = srd[j]
        rcd[z] = scd[z]
        return out

    def degree_middle(copies):
        for copy in copies:
            copy.wait_recv()
        lane = lax.broadcasted_iota(jnp.int32, (8, TB), 0).astype(F32)

        def masks(jj, _):
            for x in range(2):
                for s in range(CAP):
                    i = 8 + x * CAP + s
                    rid = jnp.broadcast_to(rrd[jj, i : i + 1], (8, TB))
                    for q in range(GT):
                        mk[x, jj, s, q] = jnp.where(rid == float(q), 1.0, 0.0)
            return 0

        lax.fori_loop(0, 8, masks, 0)

        def total(x):
            acc = jnp.zeros((8, TB), F32)
            for jj in range(8):
                for s in range(CAP):
                    val = rrd[jj, pl.ds(x * CAP + s, 1)]
                    rid = rrd[jj, pl.ds(8 + x * CAP + s, 1)]
                    acc = acc + jnp.where(rid == lane, val, 0.0)
            return acc

        first, second = total(0), total(1)
        mine = jnp.where(xl == 0, first, second)
        sxld[...] = jnp.where(xl == 0, second, first)
        s1 = send(sxld, rxld, col_dev(oxl, j))

        def csum_of(x):
            return sum(rcd[zz, x * 8 : x * 8 + 8] for zz in range(4))

        first, second = csum_of(0), csum_of(1)
        cmine = jnp.where(xh == 0, first, second)
        sxhd[...] = jnp.where(xh == 0, second, first)
        s2 = send(sxhd, rxhd, row_dev(z, oxh))
        deg[...] = mine + cmine
        return s1, s2

    def degree_end(copies):
        for copy in copies:
            copy.wait_recv()
        deg[...] = 0.5 * (deg[...] + rxld[...] + rxhd[...])

    def products(ph):
        def body(i, top):
            out = []
            for u in range(4):
                t = i * 4 + u
                tile = tiles[t]
                out.append(
                    (dot_t(colp[ph][tab[COLS + t]], tile), dot_n(rowp[ph][tab[ROWS + t]], tile))
                )
            for u in range(4):
                t = i * 4 + u
                prod[t] = out[u][0]
                total = out[u][1] + chain[tab[PREV + t]]
                chain[t] = total
                top = jnp.maximum(top, jnp.maximum(largest(out[u][0]), largest(total)))
            return top

        return lax.fori_loop(0, NT // 4, body, jnp.zeros((8, TB), F32))

    class Scatter:
        def __init__(self, p, h):
            self.p = p = p * NH + h
            self.h = h
            top = spread(products(p))
            rate = (STEPS / top)[:1]
            unit[p] = top * (1.0 / STEPS)
            runit[p, j] = unit[p]
            zunit[p, z] = unit[p]
            self.rcopies, self.ccopies = [], []
            for d in (2, 3, 4, 5, 6, 7, 1):
                j_ = (y + d // 2) % 4 * 2 + (c + d) % 2
                self.rcopies.append(send(unit.at[p], runit.at[p, j], col_dev(xl, j_)))
            for d in (1, 3, 2):
                self.ccopies.append(send(unit.at[p], zunit.at[p, z], row_dev((z + d) % 4, xh)))

            def col_body(i, _):
                for x in range(2):
                    for q in range(GT):
                        scol[p, i, x, q] = code(chain[tab[LAST + (i * 2 + x) * GT + q]], rate)
                return 0

            lax.fori_loop(0, 4, col_body, 0)
            for d in (1, 3, 2):
                self.ccopies.append(
                    send(scol.at[p, (z + d) % 4], rcol.at[p, z], row_dev((z + d) % 4, xh))
                )

            def row_body(jj, _):
                for x in range(2):
                    for s in range(CAP):
                        srow[p, jj, x, s] = code(prod[tab[SLOT + (x * 8 + jj) * CAP + s]], rate)
                return 0

            lax.fori_loop(0, 8, row_body, 0)
            for d in (2, 3, 6, 7, 4, 5, 1):
                j_ = (y + d // 2) % 4 * 2 + (c + d) % 2
                self.rcopies.append(send(srow.at[p, j_], rrow.at[p, j], col_dev(xl, j_)))
            rcol[p, z] = scol[p, z]
            rrow[p, j] = srow[p, j]

        def middle(self):
            p, h = self.p, self.h
            for copy in self.ccopies:
                copy.wait_recv()

            def col_sum(x, q):
                total = plain(rcol[p, 0, x, q]) * zunit[p, 0, 0:1]
                for zz in range(1, 4):
                    total = total + plain(rcol[p, zz, x, q]) * zunit[p, zz, 0:1]
                return total

            def other_col(q, top):
                total = col_sum(oxh, q)
                acol[h, q] = total
                return jnp.maximum(top, largest(total))

            top = spread(lax.fori_loop(0, GT, other_col, jnp.zeros((8, TB), F32)))
            xhu[p] = top * (1.0 / STEPS)
            u2 = send(xhu.at[p], rxhu.at[p], row_dev(z, oxh))
            rate = (STEPS / top)[:1]

            def code_col(q, _):
                sxh[p, q] = code(acol[h, q], rate)
                return 0

            lax.fori_loop(0, GT, code_col, 0)
            s2 = send(sxh.at[p], rxh.at[p], row_dev(z, oxh))

            for copy in self.rcopies:
                copy.wait_recv()

            def row_sum(x):
                def chunk(kc, top):
                    rows = pl.ds(pl.multiple_of(kc * 16, 16), 16)

                    def source(jj, accs):
                        accs = list(accs)
                        factor = runit[p, jj]
                        for s in range(CAP):
                            data = plain(rrow[p, jj, x, s, rows]).reshape(2, 8, TB) * factor[None]
                            for q in range(GT):
                                accs[q] = accs[q] + data * mk[x, jj, s, q][None]
                        return tuple(accs)

                    accs = lax.fori_loop(
                        0, 8, source, tuple(jnp.zeros((2, 8, TB), F32) for _ in range(GT))
                    )
                    for q in range(GT):
                        value = accs[q].reshape(16, TB)
                        arow[h, q, rows] = value
                        top = jnp.maximum(top, largest(value))
                    return top

                return lax.fori_loop(0, KH // 16, chunk, jnp.zeros((8, TB), F32))

            top = spread(row_sum(oxl))
            xlu[p] = top * (1.0 / STEPS)
            u1 = send(xlu.at[p], rxlu.at[p], col_dev(oxl, j))
            rate = (STEPS / top)[:1]

            def code_row(q, _):
                sxl[p, q] = code(arow[h, q], rate)
                return 0

            lax.fori_loop(0, GT, code_row, 0)
            s1 = send(sxl.at[p], rxl.at[p], col_dev(oxl, j))
            row_sum(xl)

            def own_col(q, _):
                acol[h, q] = col_sum(xh, q)
                return 0

            lax.fori_loop(0, GT, own_col, 0)
            self.last = (u2, s2, u1, s1)

        def end(self):
            for copy in self.last:
                copy.wait_recv()

        def symmetric(self, q):
            p, h = self.p, self.h
            total = arow[h, q] + acol[h, q]
            total = total + plain(rxl[p, q]) * rxlu[p, 0:1] + plain(rxh[p, q]) * rxhu[p, 0:1]
            return 0.5 * total

    class Sum:
        def __init__(self, n, value):
            self.n = n
            sum_a[n, col] = jnp.concatenate([value[: K // 2], value[K // 2 :]], axis=1)
            self.copies = [
                send(sum_a.at[n, col], sum_a.at[n, col], (row, (col + d) % N_COL))
                for d in range(1, N_COL)
            ]

        def middle(self):
            n = self.n
            for copy in self.copies:
                copy.wait_recv()
            total = sum_a[n, 0]
            for r in range(1, N_COL):
                total = total + sum_a[n, r]
            sum_b[n, row] = total
            self.copies = [
                send(sum_b.at[n, row], sum_b.at[n, row], ((row + d) % N_ROW, col))
                for d in range(1, N_ROW)
            ]

        def end(self):
            n = self.n
            for copy in self.copies:
                copy.wait_recv()
            total = sum_b[n, 0]
            for r in range(1, N_ROW):
                total = total + sum_b[n, r]
            total = total * (1.0 / NN)
            return jnp.concatenate([total[:, :K], total[:, K:]], axis=0)

    prod[NT] = jnp.zeros((KH, TB), F32)
    chain[NT] = jnp.zeros((KH, TB), F32)
    pl.semaphore_wait(barrier, N_ROW - 1 + N_COL - 1)
    gathers = [
        Gather(h, lambda q, h=h: v_ref[vecs(h), lanes(q)]) for h in range(NH)
    ]
    load.wait()
    dcopies = degree_start()
    for g in gathers:
        g.across()
    for g in gathers:
        g.relay()
    scatters = []
    for h in range(NH):
        gathers[h].end()
        scatters.append(Scatter(0, h))
    dlast = degree_middle(dcopies)
    for s in scatters:
        s.middle()
    degree_end(dlast)
    gathers = []
    for h in range(NH):
        s = scatters[h]
        s.end()
        for q in range(GT):
            v = v_ref[vecs(h), lanes(q)]
            image = deg[q : q + 1] * v - s.symmetric(q)
            f1[vecs(h), lanes(q)] = (image - CENTER * v) / HALF_WIDTH
        gathers.append(Gather(NH + h, lambda q, h=h: f1[vecs(h), lanes(q)]))
    for g in gathers:
        g.across()
    for g in gathers:
        g.relay()
    scatters = []
    for h in range(NH):
        gathers[h].end()
        scatters.append(Scatter(1, h))
    for s in scatters:
        s.middle()
    gathers = []
    for h in range(NH):
        s = scatters[h]
        s.end()
        for q in range(GT):
            v = f1[vecs(h), lanes(q)]
            image = deg[q : q + 1] * v - s.symmetric(q)
            f_ref[vecs(h), lanes(q)] = (
                2.0 * (image - CENTER * v) / HALF_WIDTH - v_ref[vecs(h), lanes(q)]
            )
        gathers.append(Gather(2 * NH + h, lambda q, h=h: f_ref[vecs(h), lanes(q)]))
    gram = jnp.zeros((K, K), F32)
    for q in range(GT):
        f = f_ref[:, lanes(q)]
        gram = gram + dot_t(f, f, precision=HIGH)
    gsum = Sum(0, gram)
    for g in gathers:
        g.across()
    diag = jnp.zeros((K, K), F32)
    for q in range(GT):
        f = f_ref[:, lanes(q)]
        diag = diag + dot_t(f, deg[q : q + 1] * f, precision=HIGH)
    gsum.middle()
    for g in gathers:
        g.relay()
    for g in gathers:
        g.end()

    def form(i, acc):
        parts = []
        for u in range(4):
            t = i * 4 + u
            left = jnp.concatenate([colp[2 * NH + h][tab[COLS + t]] for h in range(NH)], axis=0)
            parts.append(dot_t(left, tiles[t]).astype(BF16))
        for u in range(4):
            t = i * 4 + u
            right = jnp.concatenate([rowp[2 * NH + h][tab[ROWS + t]] for h in range(NH)], axis=0)
            acc = acc + dot_t(parts[u], right)
        return acc

    form_w = lax.fori_loop(0, NT // 4, form, jnp.zeros((K, K), F32))
    qsum = Sum(1, diag - form_w)
    gram = gsum.end()
    sub = lax.broadcasted_iota(jnp.int32, (K, 2 * K), 0)
    lane = lax.broadcasted_iota(jnp.int32, (K, 2 * K), 1)
    eye = jnp.where(lane == sub + K, 1.0, 0.0)
    a = jnp.where(lane < K, jnp.concatenate([gram, gram], axis=1), eye)

    def eliminate(a, steps):
        for i in steps:
            inv = 1.0 / jnp.sqrt(a[i : i + 1, i : i + 1])
            pivot = a[i : i + 1] * inv
            column = jnp.where(sub[:, :1] > i, a[:, i : i + 1] * inv, 0.0)
            a = jnp.where(sub == i, pivot, a - column * pivot)
        return a

    a = eliminate(a, range(K // 2))
    qsum.middle()
    a = eliminate(a, range(K // 2, K))
    inverse = a[:, K:]
    q = qsum.end()
    half = dot_n(inverse, q, precision=HIGH)
    ray = 0.5 * (dot_t(half, inverse, precision=HIGH) + dot_t(inverse, half, precision=HIGH))
    ray_ref[...] = ray
    ritz_ref[...] = dot_n(dot_n(ray, inverse, precision=HIGH), f_ref[...], precision=HIGH)
    for copy in sent:
        copy.wait_send()


def local(tiles, tile_rows, tile_cols, start_vectors):
    smem = pl.BlockSpec(memory_space=pltpu.SMEM)
    vmem = pl.BlockSpec(memory_space=pltpu.VMEM)
    table = pl.pallas_call(
        table_kernel,
        out_shape=jax.ShapeDtypeStruct((TAB,), jnp.int32),
        in_specs=[smem, smem],
        out_specs=smem,
        scratch_shapes=[pltpu.SMEM((N_COL,), jnp.int32)],
    )(tile_rows.reshape(NT), tile_cols.reshape(NT))
    own = start_vectors.shape[1]
    V = pltpu.VMEM
    RH = 2 * NH
    return pl.pallas_call(
        main_kernel,
        out_shape=(
            jax.ShapeDtypeStruct((K, own), F32),
            jax.ShapeDtypeStruct((K, K), F32),
        ),
        in_specs=[smem, pl.BlockSpec(memory_space=pl.ANY), vmem],
        out_specs=(vmem, vmem),
        scratch_shapes=[
            V((NT, TB, TB), BF16), [V((64, KH, TB), BF16)] * PH, [V((128, KH, TB), BF16)] * PH,
            V((NT + 1, KH, TB), F32), V((NT + 1, KH, TB), F32),
            V((RH, 8, 2, CAP, KH, TB), I16), V((RH, 8, 2, CAP, KH, TB), I16),
            V((RH, 4, 2, GT, KH, TB), I16), V((RH, 4, 2, GT, KH, TB), I16),
            V((RH, GT, KH, TB), I16), V((RH, GT, KH, TB), I16),
            V((RH, GT, KH, TB), I16), V((RH, GT, KH, TB), I16),
            V((NH, GT, KH, TB), F32), V((NH, GT, KH, TB), F32),
            V((NT + 1, 8, TB), F32), V((NT + 1, 8, TB), F32),
            V((8, 16, TB), F32), V((8, 16, TB), F32),
            V((4, 16, TB), F32), V((4, 16, TB), F32),
            V((8, TB), F32), V((8, TB), F32), V((8, TB), F32), V((8, TB), F32),
            V((8, TB), F32), V((2, 8, CAP, GT, 8, TB), F32), V((K, own), F32), V((K, own), F32),
            V((2, 16, K // 2, TB), F32), V((2, 8, K // 2, TB), F32),
            V((RH, 8, TB), F32), V((RH, 8, 8, TB), F32), V((RH, 4, 8, TB), F32),
            V((RH, 8, TB), F32), V((RH, 8, TB), F32), V((RH, 8, TB), F32), V((RH, 8, TB), F32),
            pltpu.SemaphoreType.DMA((NSEM,)), pltpu.SemaphoreType.DMA((NSEM,)),
            pltpu.SemaphoreType.DMA,
        ],
        compiler_params=pltpu.CompilerParams(
            collective_id=0, has_side_effects=True, vmem_limit_bytes=48 * 1024 * 1024
        ),
    )(table, tiles.reshape(NT, TB, TB), start_vectors)


def solution(mesh):
    placed = (
        P("row", "col", None, None, None),
        P("row", "col", None),
        P("row", "col", None),
        P(None, ("row", "col")),
    )
    return jax.shard_map(
        local, mesh=mesh, in_specs=placed, out_specs=(P(None, ("row", "col")), P()), check_vma=False
    )
```

```python
import functools

import jax
import jax.numpy as jnp
from jax import lax
from jax.experimental import pallas as pl
from jax.experimental.pallas import tpu as pltpu
from jax.sharding import PartitionSpec as P

MESH = pl.DeviceIdType.MESH
F32, BF16, I16 = jnp.float32, jnp.bfloat16, jnp.int16
HIGH = lax.Precision.HIGHEST
CENTER = 1.0
HALF_WIDTH = 0.5
K = 64
TB = 128
NT = 32
CAP = 4
GT = 8
N_ROW, N_COL = 8, 16
NN = 131072
COLS, ROWS, PREV, LAST, SLOT, RID = 0, 32, 64, 96, 160, 224
TAB = 288
NH = 2
KH = K // NH
PH = 3 * NH
NSEM = 360
STEPS = 32767.0


def table_kernel(rows_ref, cols_ref, tab, count):
    def clear(i, _):
        tab[LAST + i] = NT
        tab[SLOT + i] = NT
        tab[RID + i] = -1
        return 0

    lax.fori_loop(0, 64, clear, 0)
    for g in range(N_COL):
        count[g] = 0

    def put(t, _):
        r, c = rows_ref[t], cols_ref[t]
        tab[COLS + t] = c
        tab[ROWS + t] = r
        g = r // GT
        s = count[g]
        count[g] = s + 1
        tab[SLOT + g * CAP + s] = t
        tab[RID + g * CAP + s] = r % GT
        tab[PREV + t] = tab[LAST + c]
        tab[LAST + c] = t
        return 0

    lax.fori_loop(0, NT, put, 0)


def dot_t(a, b, **kw):
    return lax.dot_general(a, b, (((1,), (1,)), ((), ())), preferred_element_type=F32, **kw)


def dot_n(a, b, **kw):
    return lax.dot_general(a, b, (((1,), (0,)), ((), ())), preferred_element_type=F32, **kw)


def spread(x):
    m = jnp.max(jnp.max(x, axis=0, keepdims=True), axis=1, keepdims=True)
    return jnp.broadcast_to(jnp.maximum(m, 1e-30), x.shape)


def largest(x):
    return jnp.max(jnp.abs(x).reshape(-1, 8, TB), axis=0)


def code(x, rate):
    return jnp.round(x * rate).astype(jnp.int32).astype(I16)


def plain(x):
    return x.astype(jnp.int32).astype(F32)


def main_kernel(
    tab, tiles_hbm, v_ref, ritz_ref, ray_ref,
    tiles, colp, rowp, prod, chain, srow, rrow, scol, rcol, sxl, rxl, sxh, rxh, arow, acol,
    rsum, csum, srd, rrd, scd, rcd, sxld, rxld, sxhd, rxhd, deg, mk, f1, f_ref,
    sum_a, sum_b, unit, runit, zunit, xlu, rxlu, xhu, rxhu, ssem, rsem, lsem,
):
    row, col = lax.axis_index("row"), lax.axis_index("col")
    z, xh = row // 2, row % 2
    xl, j = col // 8, col % 8
    y, c = j // 2, j % 2
    oxl, oxh = 1 - xl, 1 - xh

    def col_dev(xl_, j_):
        return (row, xl_ * 8 + j_)

    def row_dev(z_, xh_):
        return (z_ * 2 + xh_, col)

    barrier = pltpu.get_barrier_semaphore()
    for d in range(1, N_ROW):
        pl.semaphore_signal(barrier, inc=1, device_id=((row + d) % N_ROW, col), device_id_type=MESH)
    for d in range(1, N_COL):
        pl.semaphore_signal(barrier, inc=1, device_id=(row, (col + d) % N_COL), device_id_type=MESH)
    load = pltpu.make_async_copy(tiles_hbm, tiles, lsem)
    load.start()

    sent = []

    def send(src, dst, dev):
        k = len(sent)
        copy = pltpu.make_async_remote_copy(
            src_ref=src, dst_ref=dst, send_sem=ssem.at[k], recv_sem=rsem.at[k],
            device_id=dev, device_id_type=MESH,
        )
        sent.append(copy)
        copy.start()
        return copy

    def lanes(q):
        return slice(q * TB, (q + 1) * TB)

    def vecs(h):
        return slice(h * KH, (h + 1) * KH)

    class Gather:
        def __init__(self, ph, value_of):
            self.ph, self.cores = ph, []
            for q in range(GT):
                b = value_of(q).astype(BF16)
                colp[ph][row * GT + q] = b
                rowp[ph][col * GT + q] = b
            self.x1 = self.to_col(col, oxl, y, c)
            self.x2 = self.to_row(row, z, oxh)
            self.ys = [self.to_col(col, xl, (y + d) % 4, c) for d in (2, 1, 3)]
            self.zs = [self.to_row(row, (z + d) % 4, xh) for d in (2, 1, 3)]
            self.core(col)

        def to_col(self, b, xl_, y_, c_):
            ref = rowp[self.ph].at[pl.ds(b * GT, GT)]
            return send(ref, ref, col_dev(xl_, y_ * 2 + c_))

        def to_row(self, b, z_, xh_):
            ref = colp[self.ph].at[pl.ds(b * GT, GT)]
            return send(ref, ref, row_dev(z_, xh_))

        def core(self, b):
            self.cores.append(self.to_col(b, xl, y, 1 - c))

        def across(self):
            self.x1.wait_recv()
            b = oxl * 8 + j
            self.yf = [self.to_col(b, xl, (y + d) % 4, c) for d in (2, 1, 3)]
            self.core(b)
            self.x2.wait_recv()
            b = z * 2 + oxh
            self.zf = [self.to_row(b, (z + d) % 4, xh) for d in (2, 1, 3)]

        def relay(self):
            self.far = []
            for x, ycopies, zcopies in ((xl, self.ys, self.zs), (oxl, self.yf, self.zf)):
                for d, copy in ((1, ycopies[1]), (3, ycopies[2])):
                    copy.wait_recv()
                    self.core(x * 8 + (y + 4 - d) % 4 * 2 + c)
                self.far.append((x, ycopies[0], zcopies))

        def end(self):
            for x, yfar, zcopies in self.far:
                yfar.wait_recv()
                self.core(x * 8 + (y + 2) % 4 * 2 + c)
            for x, yfar, zcopies in self.far:
                for copy in zcopies:
                    copy.wait_recv()
            for copy in self.cores:
                copy.wait_recv()

    def degree_start():
        ones = jnp.ones((16, TB), BF16)
        rsum[NT] = jnp.zeros((8, TB), F32)
        csum[NT] = jnp.zeros((8, TB), F32)

        def body(i, _):
            sums = []
            for u in range(4):
                tile = tiles[i * 4 + u]
                sums.append((dot_t(ones, tile), dot_n(ones, tile)))
            for u in range(4):
                t = i * 4 + u
                rsum[t] = sums[u][0][:8]
                csum[t] = sums[u][1][:8] + csum[tab[PREV + t]]
            return 0

        lax.fori_loop(0, NT // 4, body, 0)

        def row_body(jj, _):
            for x in range(2):
                for s in range(CAP):
                    slot = (x * 8 + jj) * CAP + s
                    i = x * CAP + s
                    srd[jj, i : i + 1] = rsum[tab[SLOT + slot]][0:1]
                    srd[jj, 8 + i : 9 + i] = jnp.full((1, TB), tab[RID + slot].astype(F32))
            return 0

        lax.fori_loop(0, 8, row_body, 0)

        def col_body(i, _):
            for x in range(2):
                for q in range(GT):
                    n = x * GT + q
                    scd[i, n : n + 1] = csum[tab[LAST + (i * 2 + x) * GT + q]][0:1]
            return 0

        lax.fori_loop(0, 4, col_body, 0)
        out = []
        for d in range(1, 8):
            j_ = (y + d // 2) % 4 * 2 + (c + d) % 2
            out.append(send(srd.at[j_], rrd.at[j], col_dev(xl, j_)))
        for d in (1, 3, 2):
            out.append(send(scd.at[(z + d) % 4], rcd.at[z], row_dev((z + d) % 4, xh)))
        rrd[j] = srd[j]
        rcd[z] = scd[z]
        return out

    def degree_middle(copies):
        for copy in copies:
            copy.wait_recv()
        lane = lax.broadcasted_iota(jnp.int32, (8, TB), 0).astype(F32)

        def masks(jj, _):
            for x in range(2):
                for s in range(CAP):
                    i = 8 + x * CAP + s
                    rid = jnp.broadcast_to(rrd[jj, i : i + 1], (8, TB))
                    for q in range(GT):
                        mk[x, jj, s, q] = jnp.where(rid == float(q), 1.0, 0.0)
            return 0

        lax.fori_loop(0, 8, masks, 0)

        def total(x):
            acc = jnp.zeros((8, TB), F32)
            for jj in range(8):
                for s in range(CAP):
                    val = rrd[jj, pl.ds(x * CAP + s, 1)]
                    rid = rrd[jj, pl.ds(8 + x * CAP + s, 1)]
                    acc = acc + jnp.where(rid == lane, val, 0.0)
            return acc

        first, second = total(0), total(1)
        mine = jnp.where(xl == 0, first, second)
        sxld[...] = jnp.where(xl == 0, second, first)
        s1 = send(sxld, rxld, col_dev(oxl, j))

        def csum_of(x):
            return sum(rcd[zz, x * 8 : x * 8 + 8] for zz in range(4))

        first, second = csum_of(0), csum_of(1)
        cmine = jnp.where(xh == 0, first, second)
        sxhd[...] = jnp.where(xh == 0, second, first)
        s2 = send(sxhd, rxhd, row_dev(z, oxh))
        deg[...] = mine + cmine
        return s1, s2

    def degree_end(copies):
        for copy in copies:
            copy.wait_recv()
        deg[...] = 0.5 * (deg[...] + rxld[...] + rxhd[...])

    def products(ph):
        def body(i, top):
            out = []
            for u in range(4):
                t = i * 4 + u
                tile = tiles[t]
                out.append(
                    (dot_t(colp[ph][tab[COLS + t]], tile), dot_n(rowp[ph][tab[ROWS + t]], tile))
                )
            for u in range(4):
                t = i * 4 + u
                prod[t] = out[u][0]
                total = out[u][1] + chain[tab[PREV + t]]
                chain[t] = total
                top = jnp.maximum(top, jnp.maximum(largest(out[u][0]), largest(total)))
            return top

        return lax.fori_loop(0, NT // 4, body, jnp.zeros((8, TB), F32))

    class Scatter:
        def __init__(self, p, h):
            self.p = p = p * NH + h
            self.h = h
            top = spread(products(p))
            rate = (STEPS / top)[:1]
            unit[p] = top * (1.0 / STEPS)
            runit[p, j] = unit[p]
            zunit[p, z] = unit[p]
            self.rcopies, self.ccopies = [], []
            for d in (2, 3, 4, 5, 6, 7, 1):
                j_ = (y + d // 2) % 4 * 2 + (c + d) % 2
                self.rcopies.append(send(unit.at[p], runit.at[p, j], col_dev(xl, j_)))
            for d in (1, 3, 2):
                self.ccopies.append(send(unit.at[p], zunit.at[p, z], row_dev((z + d) % 4, xh)))

            def col_body(i, _):
                for x in range(2):
                    for q in range(GT):
                        scol[p, i, x, q] = code(chain[tab[LAST + (i * 2 + x) * GT + q]], rate)
                return 0

            lax.fori_loop(0, 4, col_body, 0)
            for d in (2, 1, 3):
                self.ccopies.append(
                    send(scol.at[p, (z + d) % 4], rcol.at[p, z], row_dev((z + d) % 4, xh))
                )

            def row_body(jj, _):
                for x in range(2):
                    for s in range(CAP):
                        srow[p, jj, x, s] = code(prod[tab[SLOT + (x * 8 + jj) * CAP + s]], rate)
                return 0

            lax.fori_loop(0, 8, row_body, 0)
            for d in (4, 5, 2, 3, 6, 7, 1):
                j_ = (y + d // 2) % 4 * 2 + (c + d) % 2
                self.rcopies.append(send(srow.at[p, j_], rrow.at[p, j], col_dev(xl, j_)))
            rcol[p, z] = scol[p, z]
            rrow[p, j] = srow[p, j]

        def middle(self):
            p, h = self.p, self.h
            for copy in self.ccopies:
                copy.wait_recv()

            def col_sum(x, q):
                total = plain(rcol[p, 0, x, q]) * zunit[p, 0, 0:1]
                for zz in range(1, 4):
                    total = total + plain(rcol[p, zz, x, q]) * zunit[p, zz, 0:1]
                return total

            def other_col(q, top):
                total = col_sum(oxh, q)
                acol[h, q] = total
                return jnp.maximum(top, largest(total))

            top = spread(lax.fori_loop(0, GT, other_col, jnp.zeros((8, TB), F32)))
            xhu[p] = top * (1.0 / STEPS)
            u2 = send(xhu.at[p], rxhu.at[p], row_dev(z, oxh))
            rate = (STEPS / top)[:1]

            def code_col(q, _):
                sxh[p, q] = code(acol[h, q], rate)
                return 0

            lax.fori_loop(0, GT, code_col, 0)
            s2 = send(sxh.at[p], rxh.at[p], row_dev(z, oxh))

            for copy in self.rcopies:
                copy.wait_recv()

            def row_sum(x):
                def chunk(kc, top):
                    rows = pl.ds(pl.multiple_of(kc * 16, 16), 16)

                    def source(jj, accs):
                        accs = list(accs)
                        factor = runit[p, jj]
                        for s in range(CAP):
                            data = plain(rrow[p, jj, x, s, rows]).reshape(2, 8, TB) * factor[None]
                            for q in range(GT):
                                accs[q] = accs[q] + data * mk[x, jj, s, q][None]
                        return tuple(accs)

                    accs = lax.fori_loop(
                        0, 8, source, tuple(jnp.zeros((2, 8, TB), F32) for _ in range(GT))
                    )
                    for q in range(GT):
                        value = accs[q].reshape(16, TB)
                        arow[h, q, rows] = value
                        top = jnp.maximum(top, largest(value))
                    return top

                return lax.fori_loop(0, KH // 16, chunk, jnp.zeros((8, TB), F32))

            top = spread(row_sum(oxl))
            xlu[p] = top * (1.0 / STEPS)
            u1 = send(xlu.at[p], rxlu.at[p], col_dev(oxl, j))
            rate = (STEPS / top)[:1]

            def code_row(q, _):
                sxl[p, q] = code(arow[h, q], rate)
                return 0

            lax.fori_loop(0, GT, code_row, 0)
            s1 = send(sxl.at[p], rxl.at[p], col_dev(oxl, j))
            row_sum(xl)

            def own_col(q, _):
                acol[h, q] = col_sum(xh, q)
                return 0

            lax.fori_loop(0, GT, own_col, 0)
            self.last = (u2, s2, u1, s1)

        def end(self):
            for copy in self.last:
                copy.wait_recv()

        def symmetric(self, q):
            p, h = self.p, self.h
            total = arow[h, q] + acol[h, q]
            total = total + plain(rxl[p, q]) * rxlu[p, 0:1] + plain(rxh[p, q]) * rxhu[p, 0:1]
            return 0.5 * total

    class Sum:
        def __init__(self, n, value):
            self.n = n
            sum_a[n, col] = jnp.concatenate([value[: K // 2], value[K // 2 :]], axis=1)
            self.copies = [
                send(sum_a.at[n, col], sum_a.at[n, col], (row, (col + d) % N_COL))
                for d in range(1, N_COL)
            ]

        def middle(self):
            n = self.n
            for copy in self.copies:
                copy.wait_recv()
            total = sum_a[n, 0]
            for r in range(1, N_COL):
                total = total + sum_a[n, r]
            sum_b[n, row] = total
            self.copies = [
                send(sum_b.at[n, row], sum_b.at[n, row], ((row + d) % N_ROW, col))
                for d in range(1, N_ROW)
            ]

        def end(self):
            n = self.n
            for copy in self.copies:
                copy.wait_recv()
            total = sum_b[n, 0]
            for r in range(1, N_ROW):
                total = total + sum_b[n, r]
            total = total * (1.0 / NN)
            return jnp.concatenate([total[:, :K], total[:, K:]], axis=0)

    prod[NT] = jnp.zeros((KH, TB), F32)
    chain[NT] = jnp.zeros((KH, TB), F32)
    pl.semaphore_wait(barrier, N_ROW - 1 + N_COL - 1)
    gathers = [
        Gather(h, lambda q, h=h: v_ref[vecs(h), lanes(q)]) for h in range(NH)
    ]
    for g in gathers:
        g.across()
    load.wait()
    dcopies = degree_start()
    scatters = []
    for h in range(NH):
        gathers[h].relay()
        gathers[h].end()
        scatters.append(Scatter(0, h))
    dlast = degree_middle(dcopies)
    gathers = []
    for h in range(NH):
        s = scatters[h]
        s.middle()
        if h == 0:
            degree_end(dlast)
        else:
            gathers[h - 1].across()
        s.end()
        for q in range(GT):
            v = v_ref[vecs(h), lanes(q)]
            image = deg[q : q + 1] * v - s.symmetric(q)
            f1[vecs(h), lanes(q)] = (image - CENTER * v) / HALF_WIDTH
        gathers.append(Gather(NH + h, lambda q, h=h: f1[vecs(h), lanes(q)]))
    gathers[-1].across()
    scatters = []
    for h in range(NH):
        gathers[h].relay()
        gathers[h].end()
        scatters.append(Scatter(1, h))
    gathers = []
    for h in range(NH):
        s = scatters[h]
        s.middle()
        if h > 0:
            gathers[h - 1].across()
        s.end()
        for q in range(GT):
            v = f1[vecs(h), lanes(q)]
            image = deg[q : q + 1] * v - s.symmetric(q)
            f_ref[vecs(h), lanes(q)] = (
                2.0 * (image - CENTER * v) / HALF_WIDTH - v_ref[vecs(h), lanes(q)]
            )
        gathers.append(Gather(2 * NH + h, lambda q, h=h: f_ref[vecs(h), lanes(q)]))
    gram = jnp.zeros((K, K), F32)
    for q in range(GT):
        f = f_ref[:, lanes(q)]
        gram = gram + dot_t(f, f, precision=HIGH)
    gsum = Sum(0, gram)
    gathers[-1].across()
    diag = jnp.zeros((K, K), F32)
    for q in range(GT):
        f = f_ref[:, lanes(q)]
        diag = diag + dot_t(f, deg[q : q + 1] * f, precision=HIGH)
    for g in gathers:
        g.relay()
    gsum.middle()
    for g in gathers:
        g.end()

    def form(i, acc):
        parts = []
        for u in range(4):
            t = i * 4 + u
            left = jnp.concatenate([colp[2 * NH + h][tab[COLS + t]] for h in range(NH)], axis=0)
            parts.append(dot_t(left, tiles[t]).astype(BF16))
        for u in range(4):
            t = i * 4 + u
            right = jnp.concatenate([rowp[2 * NH + h][tab[ROWS + t]] for h in range(NH)], axis=0)
            acc = acc + dot_t(parts[u], right)
        return acc

    form_w = lax.fori_loop(0, NT // 4, form, jnp.zeros((K, K), F32))
    qsum = Sum(1, diag - form_w)
    gram = gsum.end()
    sub = lax.broadcasted_iota(jnp.int32, (K, 2 * K), 0)
    lane = lax.broadcasted_iota(jnp.int32, (K, 2 * K), 1)
    eye = jnp.where(lane == sub + K, 1.0, 0.0)
    a = jnp.where(lane < K, jnp.concatenate([gram, gram], axis=1), eye)

    def eliminate(a, steps):
        for i in steps:
            inv = 1.0 / jnp.sqrt(a[i : i + 1, i : i + 1])
            pivot = a[i : i + 1] * inv
            column = jnp.where(sub[:, :1] > i, a[:, i : i + 1] * inv, 0.0)
            a = jnp.where(sub == i, pivot, a - column * pivot)
        return a

    a = eliminate(a, range(K // 2))
    qsum.middle()
    a = eliminate(a, range(K // 2, K))
    inverse = a[:, K:]
    q = qsum.end()
    half = dot_n(inverse, q, precision=HIGH)
    ray = 0.5 * (dot_t(half, inverse, precision=HIGH) + dot_t(inverse, half, precision=HIGH))
    ray_ref[...] = ray
    ritz_ref[...] = dot_n(dot_n(ray, inverse, precision=HIGH), f_ref[...], precision=HIGH)
    for copy in sent:
        copy.wait_send()


def local(tiles, tile_rows, tile_cols, start_vectors):
    smem = pl.BlockSpec(memory_space=pltpu.SMEM)
    vmem = pl.BlockSpec(memory_space=pltpu.VMEM)
    table = pl.pallas_call(
        table_kernel,
        out_shape=jax.ShapeDtypeStruct((TAB,), jnp.int32),
        in_specs=[smem, smem],
        out_specs=smem,
        scratch_shapes=[pltpu.SMEM((N_COL,), jnp.int32)],
    )(tile_rows.reshape(NT), tile_cols.reshape(NT))
    own = start_vectors.shape[1]
    V = pltpu.VMEM
    RH = 2 * NH
    return pl.pallas_call(
        main_kernel,
        out_shape=(
            jax.ShapeDtypeStruct((K, own), F32),
            jax.ShapeDtypeStruct((K, K), F32),
        ),
        in_specs=[smem, pl.BlockSpec(memory_space=pl.ANY), vmem],
        out_specs=(vmem, vmem),
        scratch_shapes=[
            V((NT, TB, TB), BF16), [V((64, KH, TB), BF16)] * PH, [V((128, KH, TB), BF16)] * PH,
            V((NT + 1, KH, TB), F32), V((NT + 1, KH, TB), F32),
            V((RH, 8, 2, CAP, KH, TB), I16), V((RH, 8, 2, CAP, KH, TB), I16),
            V((RH, 4, 2, GT, KH, TB), I16), V((RH, 4, 2, GT, KH, TB), I16),
            V((RH, GT, KH, TB), I16), V((RH, GT, KH, TB), I16),
            V((RH, GT, KH, TB), I16), V((RH, GT, KH, TB), I16),
            V((NH, GT, KH, TB), F32), V((NH, GT, KH, TB), F32),
            V((NT + 1, 8, TB), F32), V((NT + 1, 8, TB), F32),
            V((8, 16, TB), F32), V((8, 16, TB), F32),
            V((4, 16, TB), F32), V((4, 16, TB), F32),
            V((8, TB), F32), V((8, TB), F32), V((8, TB), F32), V((8, TB), F32),
            V((8, TB), F32), V((2, 8, CAP, GT, 8, TB), F32), V((K, own), F32), V((K, own), F32),
            V((2, 16, K // 2, TB), F32), V((2, 8, K // 2, TB), F32),
            V((RH, 8, TB), F32), V((RH, 8, 8, TB), F32), V((RH, 4, 8, TB), F32),
            V((RH, 8, TB), F32), V((RH, 8, TB), F32), V((RH, 8, TB), F32), V((RH, 8, TB), F32),
            pltpu.SemaphoreType.DMA((NSEM,)), pltpu.SemaphoreType.DMA((NSEM,)),
            pltpu.SemaphoreType.DMA,
        ],
        compiler_params=pltpu.CompilerParams(
            collective_id=0, has_side_effects=True, vmem_limit_bytes=48 * 1024 * 1024
        ),
    )(table, tiles.reshape(NT, TB, TB), start_vectors)


def solution(mesh):
    placed = (
        P("row", "col", None, None, None),
        P("row", "col", None),
        P("row", "col", None),
        P(None, ("row", "col")),
    )
    return jax.shard_map(
        local, mesh=mesh, in_specs=placed, out_specs=(P(None, ("row", "col")), P()), check_vma=False
    )
```

```python
import functools

import jax
import jax.numpy as jnp
from jax import lax
from jax.experimental import pallas as pl
from jax.experimental.pallas import tpu as pltpu
from jax.sharding import PartitionSpec as P

MESH = pl.DeviceIdType.MESH
F32, BF16, I16 = jnp.float32, jnp.bfloat16, jnp.int16
HIGH = lax.Precision.HIGHEST
CENTER = 1.0
HALF_WIDTH = 0.5
K = 64
TB = 128
NT = 32
CAP = 4
GT = 8
N_ROW, N_COL = 8, 16
NN = 131072
COLS, ROWS, PREV, LAST, SLOT, RID = 0, 32, 64, 96, 160, 224
TAB = 288
NH = 2
KH = K // NH
PH = 3 * NH
NSEM = 360
STEPS = 32767.0


def table_kernel(rows_ref, cols_ref, tab, count):
    def clear(i, _):
        tab[LAST + i] = NT
        tab[SLOT + i] = NT
        tab[RID + i] = -1
        return 0

    lax.fori_loop(0, 64, clear, 0)
    for g in range(N_COL):
        count[g] = 0

    def put(t, _):
        r, c = rows_ref[t], cols_ref[t]
        tab[COLS + t] = c
        tab[ROWS + t] = r
        g = r // GT
        s = count[g]
        count[g] = s + 1
        tab[SLOT + g * CAP + s] = t
        tab[RID + g * CAP + s] = r % GT
        tab[PREV + t] = tab[LAST + c]
        tab[LAST + c] = t
        return 0

    lax.fori_loop(0, NT, put, 0)


def dot_t(a, b, **kw):
    return lax.dot_general(a, b, (((1,), (1,)), ((), ())), preferred_element_type=F32, **kw)


def dot_n(a, b, **kw):
    return lax.dot_general(a, b, (((1,), (0,)), ((), ())), preferred_element_type=F32, **kw)


def spread(x):
    m = jnp.max(jnp.max(x, axis=0, keepdims=True), axis=1, keepdims=True)
    return jnp.broadcast_to(jnp.maximum(m, 1e-30), x.shape)


def largest(x):
    return jnp.max(jnp.abs(x).reshape(-1, 8, TB), axis=0)


def code(x, rate):
    return jnp.round(x * rate).astype(jnp.int32).astype(I16)


def plain(x):
    return x.astype(jnp.int32).astype(F32)


def main_kernel(
    tab, tiles_hbm, v_hbm, ritz_ref, ray_ref,
    tiles, v_ref, colp, rowp, prod, chain, srow, rrow, scol, rcol, sxl, rxl, sxh, rxh, arow, acol,
    rsum, csum, srd, rrd, scd, rcd, sxld, rxld, sxhd, rxhd, deg, mk, f1, f_ref,
    sum_a, sum_b, unit, runit, zunit, xlu, rxlu, xhu, rxhu, ssem, rsem, lsem,
):
    row, col = lax.axis_index("row"), lax.axis_index("col")
    z, xh = row // 2, row % 2
    xl, j = col // 8, col % 8
    y, c = j // 2, j % 2
    oxl, oxh = 1 - xl, 1 - xh

    def col_dev(xl_, j_):
        return (row, xl_ * 8 + j_)

    def row_dev(z_, xh_):
        return (z_ * 2 + xh_, col)

    barrier = pltpu.get_barrier_semaphore()
    for d in range(1, N_ROW):
        pl.semaphore_signal(barrier, inc=1, device_id=((row + d) % N_ROW, col), device_id_type=MESH)
    for d in range(1, N_COL):
        pl.semaphore_signal(barrier, inc=1, device_id=(row, (col + d) % N_COL), device_id_type=MESH)
    load_v = pltpu.make_async_copy(v_hbm, v_ref, lsem.at[0])
    load_v.start()
    load = pltpu.make_async_copy(tiles_hbm, tiles, lsem.at[1])
    load.start()

    sent = []

    def send(src, dst, dev):
        k = len(sent)
        copy = pltpu.make_async_remote_copy(
            src_ref=src, dst_ref=dst, send_sem=ssem.at[k], recv_sem=rsem.at[k],
            device_id=dev, device_id_type=MESH,
        )
        sent.append(copy)
        copy.start()
        return copy

    def lanes(q):
        return slice(q * TB, (q + 1) * TB)

    def vecs(h):
        return slice(h * KH, (h + 1) * KH)

    class Gather:
        def __init__(self, ph, value_of, now=True):
            self.ph, self.cores = ph, []
            for q in range(GT):
                b = value_of(q).astype(BF16)
                colp[ph][row * GT + q] = b
                rowp[ph][col * GT + q] = b
            self.x1 = self.to_col(col, oxl, y, c)
            self.x2 = self.to_row(row, z, oxh)
            if now:
                self.near()

        def near(self):
            self.ys = [self.to_col(col, xl, (y + d) % 4, c) for d in (2, 1, 3)]
            self.zs = [self.to_row(row, (z + d) % 4, xh) for d in (2, 1, 3)]
            self.core(col)

        def to_col(self, b, xl_, y_, c_):
            ref = rowp[self.ph].at[pl.ds(b * GT, GT)]
            return send(ref, ref, col_dev(xl_, y_ * 2 + c_))

        def to_row(self, b, z_, xh_):
            ref = colp[self.ph].at[pl.ds(b * GT, GT)]
            return send(ref, ref, row_dev(z_, xh_))

        def core(self, b):
            self.cores.append(self.to_col(b, xl, y, 1 - c))

        def across(self):
            self.x1.wait_recv()
            b = oxl * 8 + j
            self.yf = [self.to_col(b, xl, (y + d) % 4, c) for d in (2, 1, 3)]
            self.core(b)
            self.x2.wait_recv()
            b = z * 2 + oxh
            self.zf = [self.to_row(b, (z + d) % 4, xh) for d in (2, 1, 3)]

        def relay(self):
            self.far = []
            for x, ycopies, zcopies in ((xl, self.ys, self.zs), (oxl, self.yf, self.zf)):
                for d, copy in ((1, ycopies[1]), (3, ycopies[2])):
                    copy.wait_recv()
                    self.core(x * 8 + (y + 4 - d) % 4 * 2 + c)
                self.far.append((x, ycopies[0], zcopies))

        def end(self):
            for x, yfar, zcopies in self.far:
                yfar.wait_recv()
                self.core(x * 8 + (y + 2) % 4 * 2 + c)
            for x, yfar, zcopies in self.far:
                for copy in zcopies:
                    copy.wait_recv()
            for copy in self.cores:
                copy.wait_recv()

    def degree_start():
        ones = jnp.ones((16, TB), BF16)
        rsum[NT] = jnp.zeros((8, TB), F32)
        csum[NT] = jnp.zeros((8, TB), F32)

        def body(i, _):
            sums = []
            for u in range(4):
                tile = tiles[i * 4 + u]
                sums.append((dot_t(ones, tile), dot_n(ones, tile)))
            for u in range(4):
                t = i * 4 + u
                rsum[t] = sums[u][0][:8]
                csum[t] = sums[u][1][:8] + csum[tab[PREV + t]]
            return 0

        lax.fori_loop(0, NT // 4, body, 0)

        def row_body(jj, _):
            for x in range(2):
                for s in range(CAP):
                    slot = (x * 8 + jj) * CAP + s
                    i = x * CAP + s
                    srd[jj, i : i + 1] = rsum[tab[SLOT + slot]][0:1]
                    srd[jj, 8 + i : 9 + i] = jnp.full((1, TB), tab[RID + slot].astype(F32))
            return 0

        lax.fori_loop(0, 8, row_body, 0)

        def col_body(i, _):
            for x in range(2):
                for q in range(GT):
                    n = x * GT + q
                    scd[i, n : n + 1] = csum[tab[LAST + (i * 2 + x) * GT + q]][0:1]
            return 0

        lax.fori_loop(0, 4, col_body, 0)
        out = []
        for d in range(1, 8):
            j_ = (y + d // 2) % 4 * 2 + (c + d) % 2
            out.append(send(srd.at[j_], rrd.at[j], col_dev(xl, j_)))
        for d in (1, 3, 2):
            out.append(send(scd.at[(z + d) % 4], rcd.at[z], row_dev((z + d) % 4, xh)))
        rrd[j] = srd[j]
        rcd[z] = scd[z]
        return out

    def degree_middle(copies):
        for copy in copies:
            copy.wait_recv()
        lane = lax.broadcasted_iota(jnp.int32, (8, TB), 0).astype(F32)

        def masks(jj, _):
            for x in range(2):
                for s in range(CAP):
                    i = 8 + x * CAP + s
                    rid = jnp.broadcast_to(rrd[jj, i : i + 1], (8, TB))
                    for q in range(GT):
                        mk[x, jj, s, q] = jnp.where(rid == float(q), 1.0, 0.0)
            return 0

        lax.fori_loop(0, 8, masks, 0)

        def total(x):
            acc = jnp.zeros((8, TB), F32)
            for jj in range(8):
                for s in range(CAP):
                    val = rrd[jj, pl.ds(x * CAP + s, 1)]
                    rid = rrd[jj, pl.ds(8 + x * CAP + s, 1)]
                    acc = acc + jnp.where(rid == lane, val, 0.0)
            return acc

        first, second = total(0), total(1)
        mine = jnp.where(xl == 0, first, second)
        sxld[...] = jnp.where(xl == 0, second, first)
        s1 = send(sxld, rxld, col_dev(oxl, j))

        def csum_of(x):
            return sum(rcd[zz, x * 8 : x * 8 + 8] for zz in range(4))

        first, second = csum_of(0), csum_of(1)
        cmine = jnp.where(xh == 0, first, second)
        sxhd[...] = jnp.where(xh == 0, second, first)
        s2 = send(sxhd, rxhd, row_dev(z, oxh))
        deg[...] = mine + cmine
        return s1, s2

    def degree_end(copies):
        for copy in copies:
            copy.wait_recv()
        deg[...] = 0.5 * (deg[...] + rxld[...] + rxhd[...])

    def products(ph):
        def body(i, top):
            out = []
            for u in range(4):
                t = i * 4 + u
                tile = tiles[t]
                out.append(
                    (dot_t(colp[ph][tab[COLS + t]], tile), dot_n(rowp[ph][tab[ROWS + t]], tile))
                )
            for u in range(4):
                t = i * 4 + u
                prod[t] = out[u][0]
                total = out[u][1] + chain[tab[PREV + t]]
                chain[t] = total
                top = jnp.maximum(top, jnp.maximum(largest(out[u][0]), largest(total)))
            return top

        return lax.fori_loop(0, NT // 4, body, jnp.zeros((8, TB), F32))

    class Scatter:
        def __init__(self, p, h):
            self.p = p = p * NH + h
            self.h = h
            top = spread(products(p))
            rate = (STEPS / top)[:1]
            unit[p] = top * (1.0 / STEPS)
            runit[p, j] = unit[p]
            zunit[p, z] = unit[p]
            self.rcopies, self.ccopies = [], []
            for d in (2, 3, 4, 5, 6, 7, 1):
                j_ = (y + d // 2) % 4 * 2 + (c + d) % 2
                self.rcopies.append(send(unit.at[p], runit.at[p, j], col_dev(xl, j_)))
            for d in (1, 3, 2):
                self.ccopies.append(send(unit.at[p], zunit.at[p, z], row_dev((z + d) % 4, xh)))

            def col_body(i, _):
                for x in range(2):
                    for q in range(GT):
                        scol[p, i, x, q] = code(chain[tab[LAST + (i * 2 + x) * GT + q]], rate)
                return 0

            lax.fori_loop(0, 4, col_body, 0)
            for d in (2, 1, 3):
                self.ccopies.append(
                    send(scol.at[p, (z + d) % 4], rcol.at[p, z], row_dev((z + d) % 4, xh))
                )

            def row_body(jj, _):
                for x in range(2):
                    for s in range(CAP):
                        srow[p, jj, x, s] = code(prod[tab[SLOT + (x * 8 + jj) * CAP + s]], rate)
                return 0

            lax.fori_loop(0, 8, row_body, 0)
            for d in (4, 5, 2, 3, 6, 7, 1):
                j_ = (y + d // 2) % 4 * 2 + (c + d) % 2
                self.rcopies.append(send(srow.at[p, j_], rrow.at[p, j], col_dev(xl, j_)))
            rcol[p, z] = scol[p, z]
            rrow[p, j] = srow[p, j]

        def middle(self):
            p, h = self.p, self.h
            for copy in self.ccopies:
                copy.wait_recv()

            def col_sum(x, q):
                total = plain(rcol[p, 0, x, q]) * zunit[p, 0, 0:1]
                for zz in range(1, 4):
                    total = total + plain(rcol[p, zz, x, q]) * zunit[p, zz, 0:1]
                return total

            def other_col(q, top):
                total = col_sum(oxh, q)
                acol[h, q] = total
                return jnp.maximum(top, largest(total))

            top = spread(lax.fori_loop(0, GT, other_col, jnp.zeros((8, TB), F32)))
            xhu[p] = top * (1.0 / STEPS)
            u2 = send(xhu.at[p], rxhu.at[p], row_dev(z, oxh))
            rate = (STEPS / top)[:1]

            def code_col(q, _):
                sxh[p, q] = code(acol[h, q], rate)
                return 0

            lax.fori_loop(0, GT, code_col, 0)
            s2 = send(sxh.at[p], rxh.at[p], row_dev(z, oxh))

            for copy in self.rcopies:
                copy.wait_recv()

            def row_sum(x):
                def chunk(kc, top):
                    rows = pl.ds(pl.multiple_of(kc * 16, 16), 16)

                    def source(jj, accs):
                        accs = list(accs)
                        factor = runit[p, jj]
                        for s in range(CAP):
                            data = plain(rrow[p, jj, x, s, rows]).reshape(2, 8, TB) * factor[None]
                            for q in range(GT):
                                accs[q] = accs[q] + data * mk[x, jj, s, q][None]
                        return tuple(accs)

                    accs = lax.fori_loop(
                        0, 8, source, tuple(jnp.zeros((2, 8, TB), F32) for _ in range(GT))
                    )
                    for q in range(GT):
                        value = accs[q].reshape(16, TB)
                        arow[h, q, rows] = value
                        top = jnp.maximum(top, largest(value))
                    return top

                return lax.fori_loop(0, KH // 16, chunk, jnp.zeros((8, TB), F32))

            top = spread(row_sum(oxl))
            xlu[p] = top * (1.0 / STEPS)
            u1 = send(xlu.at[p], rxlu.at[p], col_dev(oxl, j))
            rate = (STEPS / top)[:1]

            def code_row(q, _):
                sxl[p, q] = code(arow[h, q], rate)
                return 0

            lax.fori_loop(0, GT, code_row, 0)
            s1 = send(sxl.at[p], rxl.at[p], col_dev(oxl, j))
            row_sum(xl)

            def own_col(q, _):
                acol[h, q] = col_sum(xh, q)
                return 0

            lax.fori_loop(0, GT, own_col, 0)
            self.last = (u2, s2, u1, s1)

        def end(self):
            for copy in self.last:
                copy.wait_recv()

        def symmetric(self, q):
            p, h = self.p, self.h
            total = arow[h, q] + acol[h, q]
            total = total + plain(rxl[p, q]) * rxlu[p, 0:1] + plain(rxh[p, q]) * rxhu[p, 0:1]
            return 0.5 * total

    class Sum:
        def __init__(self, n, value):
            self.n = n
            sum_a[n, col] = jnp.concatenate([value[: K // 2], value[K // 2 :]], axis=1)
            self.copies = [
                send(sum_a.at[n, col], sum_a.at[n, col], (row, (col + d) % N_COL))
                for d in range(1, N_COL)
            ]

        def middle(self):
            n = self.n
            for copy in self.copies:
                copy.wait_recv()
            total = sum_a[n, 0]
            for r in range(1, N_COL):
                total = total + sum_a[n, r]
            sum_b[n, row] = total
            self.copies = [
                send(sum_b.at[n, row], sum_b.at[n, row], ((row + d) % N_ROW, col))
                for d in range(1, N_ROW)
            ]

        def end(self):
            n = self.n
            for copy in self.copies:
                copy.wait_recv()
            total = sum_b[n, 0]
            for r in range(1, N_ROW):
                total = total + sum_b[n, r]
            total = total * (1.0 / NN)
            return jnp.concatenate([total[:, :K], total[:, K:]], axis=0)

    prod[NT] = jnp.zeros((KH, TB), F32)
    chain[NT] = jnp.zeros((KH, TB), F32)
    load_v.wait()
    pl.semaphore_wait(barrier, N_ROW - 1 + N_COL - 1)
    gathers = [
        Gather(h, lambda q, h=h: v_ref[vecs(h), lanes(q)], h == 0) for h in range(NH)
    ]
    for h in range(NH):
        gathers[h].across()
        if h + 1 < NH:
            gathers[h + 1].near()
    load.wait()
    dcopies = degree_start()
    scatters = []
    for h in range(NH):
        gathers[h].relay()
        gathers[h].end()
        scatters.append(Scatter(0, h))
    dlast = degree_middle(dcopies)
    gathers = []
    for h in range(NH):
        s = scatters[h]
        s.middle()
        if h == 0:
            degree_end(dlast)
        else:
            gathers[h - 1].across()
        s.end()
        for q in range(GT):
            v = v_ref[vecs(h), lanes(q)]
            image = deg[q : q + 1] * v - s.symmetric(q)
            f1[vecs(h), lanes(q)] = (image - CENTER * v) / HALF_WIDTH
        gathers.append(Gather(NH + h, lambda q, h=h: f1[vecs(h), lanes(q)]))
    gathers[-1].across()
    scatters = []
    for h in range(NH):
        gathers[h].relay()
        gathers[h].end()
        scatters.append(Scatter(1, h))
    gathers = []
    for h in range(NH):
        s = scatters[h]
        s.middle()
        if h > 0:
            gathers[h - 1].across()
        s.end()
        for q in range(GT):
            v = f1[vecs(h), lanes(q)]
            image = deg[q : q + 1] * v - s.symmetric(q)
            f_ref[vecs(h), lanes(q)] = (
                2.0 * (image - CENTER * v) / HALF_WIDTH - v_ref[vecs(h), lanes(q)]
            )
        gathers.append(Gather(2 * NH + h, lambda q, h=h: f_ref[vecs(h), lanes(q)]))
    gram = jnp.zeros((K, K), F32)
    for q in range(GT):
        f = f_ref[:, lanes(q)]
        gram = gram + dot_t(f, f, precision=HIGH)
    gathers[-1].across()
    gsum = Sum(0, gram)
    diag = jnp.zeros((K, K), F32)
    for q in range(GT):
        f = f_ref[:, lanes(q)]
        diag = diag + dot_t(f, deg[q : q + 1] * f, precision=HIGH)
    for g in gathers:
        g.relay()
    for g in gathers:
        g.end()
    gsum.middle()

    def form(i, acc):
        parts = []
        for u in range(4):
            t = i * 4 + u
            left = jnp.concatenate([colp[2 * NH + h][tab[COLS + t]] for h in range(NH)], axis=0)
            parts.append(dot_t(left, tiles[t]).astype(BF16))
        for u in range(4):
            t = i * 4 + u
            right = jnp.concatenate([rowp[2 * NH + h][tab[ROWS + t]] for h in range(NH)], axis=0)
            acc = acc + dot_t(parts[u], right)
        return acc

    form_w = lax.fori_loop(0, NT // 4, form, jnp.zeros((K, K), F32))
    qsum = Sum(1, diag - form_w)
    gram = gsum.end()
    sub = lax.broadcasted_iota(jnp.int32, (K, 2 * K), 0)
    lane = lax.broadcasted_iota(jnp.int32, (K, 2 * K), 1)
    eye = jnp.where(lane == sub + K, 1.0, 0.0)
    a = jnp.where(lane < K, jnp.concatenate([gram, gram], axis=1), eye)

    def eliminate(a, steps):
        for i in steps:
            square = a[i : i + 1, i : i + 1]
            inv = lax.rsqrt(square)
            inv = inv * (1.5 - 0.5 * square * inv * inv)
            pivot = a[i : i + 1] * inv
            column = jnp.where(sub[:, :1] > i, a[:, i : i + 1] * inv, 0.0)
            a = jnp.where(sub == i, pivot, a - column * pivot)
        return a

    a = eliminate(a, range(K // 2))
    qsum.middle()
    a = eliminate(a, range(K // 2, K))
    inverse = a[:, K:]
    q = qsum.end()
    half = dot_n(inverse, q, precision=HIGH)
    ray = 0.5 * (dot_t(half, inverse, precision=HIGH) + dot_t(inverse, half, precision=HIGH))
    ray_ref[...] = ray
    ritz_ref[...] = dot_n(dot_n(ray, inverse, precision=HIGH), f_ref[...], precision=HIGH)
    for copy in sent:
        copy.wait_send()


def local(tiles, tile_rows, tile_cols, start_vectors):
    smem = pl.BlockSpec(memory_space=pltpu.SMEM)
    vmem = pl.BlockSpec(memory_space=pltpu.VMEM)
    table = pl.pallas_call(
        table_kernel,
        out_shape=jax.ShapeDtypeStruct((TAB,), jnp.int32),
        in_specs=[smem, smem],
        out_specs=smem,
        scratch_shapes=[pltpu.SMEM((N_COL,), jnp.int32)],
    )(tile_rows.reshape(NT), tile_cols.reshape(NT))
    own = start_vectors.shape[1]
    V = pltpu.VMEM
    RH = 2 * NH
    return pl.pallas_call(
        main_kernel,
        out_shape=(
            jax.ShapeDtypeStruct((K, own), F32),
            jax.ShapeDtypeStruct((K, K), F32),
        ),
        in_specs=[smem, pl.BlockSpec(memory_space=pl.ANY), pl.BlockSpec(memory_space=pl.ANY)],
        out_specs=(vmem, vmem),
        scratch_shapes=[
            V((NT, TB, TB), BF16), V((K, own), F32), [V((64, KH, TB), BF16)] * PH, [V((128, KH, TB), BF16)] * PH,
            V((NT + 1, KH, TB), F32), V((NT + 1, KH, TB), F32),
            V((RH, 8, 2, CAP, KH, TB), I16), V((RH, 8, 2, CAP, KH, TB), I16),
            V((RH, 4, 2, GT, KH, TB), I16), V((RH, 4, 2, GT, KH, TB), I16),
            V((RH, GT, KH, TB), I16), V((RH, GT, KH, TB), I16),
            V((RH, GT, KH, TB), I16), V((RH, GT, KH, TB), I16),
            V((NH, GT, KH, TB), F32), V((NH, GT, KH, TB), F32),
            V((NT + 1, 8, TB), F32), V((NT + 1, 8, TB), F32),
            V((8, 16, TB), F32), V((8, 16, TB), F32),
            V((4, 16, TB), F32), V((4, 16, TB), F32),
            V((8, TB), F32), V((8, TB), F32), V((8, TB), F32), V((8, TB), F32),
            V((8, TB), F32), V((2, 8, CAP, GT, 8, TB), F32), V((K, own), F32), V((K, own), F32),
            V((2, 16, K // 2, TB), F32), V((2, 8, K // 2, TB), F32),
            V((RH, 8, TB), F32), V((RH, 8, 8, TB), F32), V((RH, 4, 8, TB), F32),
            V((RH, 8, TB), F32), V((RH, 8, TB), F32), V((RH, 8, TB), F32), V((RH, 8, TB), F32),
            pltpu.SemaphoreType.DMA((NSEM,)), pltpu.SemaphoreType.DMA((NSEM,)),
            pltpu.SemaphoreType.DMA((2,)),
        ],
        compiler_params=pltpu.CompilerParams(
            collective_id=0, has_side_effects=True, vmem_limit_bytes=48 * 1024 * 1024
        ),
    )(table, tiles.reshape(NT, TB, TB), start_vectors)


def solution(mesh):
    placed = (
        P("row", "col", None, None, None),
        P("row", "col", None),
        P("row", "col", None),
        P(None, ("row", "col")),
    )
    return jax.shard_map(
        local, mesh=mesh, in_specs=placed, out_specs=(P(None, ("row", "col")), P()), check_vma=False
    )
```

```python
import functools

import jax
import jax.numpy as jnp
from jax import lax
from jax.experimental import pallas as pl
from jax.experimental.pallas import tpu as pltpu
from jax.sharding import PartitionSpec as P

MESH = pl.DeviceIdType.MESH
F32, BF16, I16 = jnp.float32, jnp.bfloat16, jnp.int16
HIGH = lax.Precision.HIGHEST
CENTER = 1.0
HALF_WIDTH = 0.5
K = 64
TB = 128
NT = 32
CAP = 4
GT = 8
N_ROW, N_COL = 8, 16
NN = 131072
COLS, ROWS, PREV, LAST, SLOT, RID = 0, 32, 64, 96, 160, 224
TAB = 288
NH = 2
KH = K // NH
PH = 3 * NH
NSEM = 360
STEPS = 32767.0


def table_kernel(rows_ref, cols_ref, tab, count):
    def clear(i, _):
        tab[LAST + i] = NT
        tab[SLOT + i] = NT
        tab[RID + i] = -1
        return 0

    lax.fori_loop(0, 64, clear, 0)
    for g in range(N_COL):
        count[g] = 0

    def put(t, _):
        r, c = rows_ref[t], cols_ref[t]
        tab[COLS + t] = c
        tab[ROWS + t] = r
        g = r // GT
        s = count[g]
        count[g] = s + 1
        tab[SLOT + g * CAP + s] = t
        tab[RID + g * CAP + s] = r % GT
        tab[PREV + t] = tab[LAST + c]
        tab[LAST + c] = t
        return 0

    lax.fori_loop(0, NT, put, 0)


def dot_t(a, b, **kw):
    return lax.dot_general(a, b, (((1,), (1,)), ((), ())), preferred_element_type=F32, **kw)


def dot_n(a, b, **kw):
    return lax.dot_general(a, b, (((1,), (0,)), ((), ())), preferred_element_type=F32, **kw)


def spread(x):
    m = jnp.max(jnp.max(x, axis=0, keepdims=True), axis=1, keepdims=True)
    return jnp.broadcast_to(jnp.maximum(m, 1e-30), x.shape)


def largest(x):
    return jnp.max(jnp.abs(x).reshape(-1, 8, TB), axis=0)


def code(x, rate):
    return jnp.round(x * rate).astype(jnp.int32).astype(I16)


def plain(x):
    return x.astype(jnp.int32).astype(F32)


def main_kernel(
    tab, tiles_hbm, v_hbm, ritz_ref, ray_ref,
    tiles, v_ref, colp, rowp, prod, chain, srow, rrow, scol, rcol, sxl, rxl, sxh, rxh, arow, acol,
    rsum, csum, srd, rrd, scd, rcd, sxld, rxld, sxhd, rxhd, deg, mk, f1, f_ref,
    sum_a, sum_b, unit, runit, zunit, xlu, rxlu, xhu, rxhu, ssem, rsem, lsem,
):
    row, col = lax.axis_index("row"), lax.axis_index("col")
    z, xh = row // 2, row % 2
    xl, j = col // 8, col % 8
    y, c = j // 2, j % 2
    oxl, oxh = 1 - xl, 1 - xh

    def col_dev(xl_, j_):
        return (row, xl_ * 8 + j_)

    def row_dev(z_, xh_):
        return (z_ * 2 + xh_, col)

    barrier = pltpu.get_barrier_semaphore()
    for d in range(1, N_ROW):
        pl.semaphore_signal(barrier, inc=1, device_id=((row + d) % N_ROW, col), device_id_type=MESH)
    for d in range(1, N_COL):
        pl.semaphore_signal(barrier, inc=1, device_id=(row, (col + d) % N_COL), device_id_type=MESH)
    load_v = pltpu.make_async_copy(v_hbm, v_ref, lsem.at[0])
    load_v.start()
    load = pltpu.make_async_copy(tiles_hbm, tiles, lsem.at[1])
    load.start()

    sent = []

    def send(src, dst, dev):
        k = len(sent)
        copy = pltpu.make_async_remote_copy(
            src_ref=src, dst_ref=dst, send_sem=ssem.at[k], recv_sem=rsem.at[k],
            device_id=dev, device_id_type=MESH,
        )
        sent.append(copy)
        copy.start()
        return copy

    def lanes(q):
        return slice(q * TB, (q + 1) * TB)

    def vecs(h):
        return slice(h * KH, (h + 1) * KH)

    class Gather:
        def __init__(self, ph, value_of, now=True):
            self.ph, self.cores = ph, []
            for q in range(GT):
                b = value_of(q).astype(BF16)
                colp[ph][row * GT + q] = b
                rowp[ph][col * GT + q] = b
            self.x1 = self.to_col(col, oxl, y, c)
            self.x2 = self.to_row(row, z, oxh)
            if now:
                self.near()

        def near(self):
            self.ys = [self.to_col(col, xl, (y + d) % 4, c) for d in (2, 1, 3)]
            self.zs = [self.to_row(row, (z + d) % 4, xh) for d in (2, 1, 3)]
            self.core(col)

        def to_col(self, b, xl_, y_, c_):
            ref = rowp[self.ph].at[pl.ds(b * GT, GT)]
            return send(ref, ref, col_dev(xl_, y_ * 2 + c_))

        def to_row(self, b, z_, xh_):
            ref = colp[self.ph].at[pl.ds(b * GT, GT)]
            return send(ref, ref, row_dev(z_, xh_))

        def core(self, b):
            self.cores.append(self.to_col(b, xl, y, 1 - c))

        def across(self):
            self.x1.wait_recv()
            b = oxl * 8 + j
            self.yf = [self.to_col(b, xl, (y + d) % 4, c) for d in (2, 1, 3)]
            self.core(b)
            self.x2.wait_recv()
            b = z * 2 + oxh
            self.zf = [self.to_row(b, (z + d) % 4, xh) for d in (2, 1, 3)]

        def relay(self):
            self.far = []
            for x, ycopies, zcopies in ((xl, self.ys, self.zs), (oxl, self.yf, self.zf)):
                for d, copy in ((1, ycopies[1]), (3, ycopies[2])):
                    copy.wait_recv()
                    self.core(x * 8 + (y + 4 - d) % 4 * 2 + c)
                self.far.append((x, ycopies[0], zcopies))

        def end(self):
            for x, yfar, zcopies in self.far:
                yfar.wait_recv()
                self.core(x * 8 + (y + 2) % 4 * 2 + c)
            for x, yfar, zcopies in self.far:
                for copy in zcopies:
                    copy.wait_recv()
            for copy in self.cores:
                copy.wait_recv()

    def degree_start():
        ones = jnp.ones((16, TB), BF16)
        rsum[NT] = jnp.zeros((8, TB), F32)
        csum[NT] = jnp.zeros((8, TB), F32)

        def body(i, _):
            sums = []
            for u in range(4):
                tile = tiles[i * 4 + u]
                sums.append((dot_t(ones, tile), dot_n(ones, tile)))
            for u in range(4):
                t = i * 4 + u
                rsum[t] = sums[u][0][:8]
                csum[t] = sums[u][1][:8] + csum[tab[PREV + t]]
            return 0

        lax.fori_loop(0, NT // 4, body, 0)

        def row_body(jj, _):
            for x in range(2):
                for s in range(CAP):
                    slot = (x * 8 + jj) * CAP + s
                    i = x * CAP + s
                    srd[jj, i : i + 1] = rsum[tab[SLOT + slot]][0:1]
                    srd[jj, 8 + i : 9 + i] = jnp.full((1, TB), tab[RID + slot].astype(F32))
            return 0

        lax.fori_loop(0, 8, row_body, 0)

        def col_body(i, _):
            for x in range(2):
                for q in range(GT):
                    n = x * GT + q
                    scd[i, n : n + 1] = csum[tab[LAST + (i * 2 + x) * GT + q]][0:1]
            return 0

        lax.fori_loop(0, 4, col_body, 0)
        out = []
        for d in range(1, 8):
            j_ = (y + d // 2) % 4 * 2 + (c + d) % 2
            out.append(send(srd.at[j_], rrd.at[j], col_dev(xl, j_)))
        for d in (1, 3, 2):
            out.append(send(scd.at[(z + d) % 4], rcd.at[z], row_dev((z + d) % 4, xh)))
        rrd[j] = srd[j]
        rcd[z] = scd[z]
        return out

    def degree_middle(copies):
        for copy in copies:
            copy.wait_recv()
        lane = lax.broadcasted_iota(jnp.int32, (8, TB), 0).astype(F32)

        def masks(jj, _):
            for x in range(2):
                for s in range(CAP):
                    i = 8 + x * CAP + s
                    rid = jnp.broadcast_to(rrd[jj, i : i + 1], (8, TB))
                    for q in range(GT):
                        mk[x, jj, s, q] = jnp.where(rid == float(q), 1.0, 0.0)
            return 0

        lax.fori_loop(0, 8, masks, 0)

        def total(x):
            acc = jnp.zeros((8, TB), F32)
            for jj in range(8):
                for s in range(CAP):
                    val = rrd[jj, pl.ds(x * CAP + s, 1)]
                    rid = rrd[jj, pl.ds(8 + x * CAP + s, 1)]
                    acc = acc + jnp.where(rid == lane, val, 0.0)
            return acc

        first, second = total(0), total(1)
        mine = jnp.where(xl == 0, first, second)
        sxld[...] = jnp.where(xl == 0, second, first)
        s1 = send(sxld, rxld, col_dev(oxl, j))

        def csum_of(x):
            return sum(rcd[zz, x * 8 : x * 8 + 8] for zz in range(4))

        first, second = csum_of(0), csum_of(1)
        cmine = jnp.where(xh == 0, first, second)
        sxhd[...] = jnp.where(xh == 0, second, first)
        s2 = send(sxhd, rxhd, row_dev(z, oxh))
        deg[...] = mine + cmine
        return s1, s2

    def degree_end(copies):
        for copy in copies:
            copy.wait_recv()
        deg[...] = 0.5 * (deg[...] + rxld[...] + rxhd[...])

    def products(ph):
        def body(i, top):
            out = []
            for u in range(4):
                t = i * 4 + u
                tile = tiles[t]
                out.append(
                    (dot_t(colp[ph][tab[COLS + t]], tile), dot_n(rowp[ph][tab[ROWS + t]], tile))
                )
            for u in range(4):
                t = i * 4 + u
                prod[t] = out[u][0]
                total = out[u][1] + chain[tab[PREV + t]]
                chain[t] = total
                top = jnp.maximum(top, jnp.maximum(largest(out[u][0]), largest(total)))
            return top

        return lax.fori_loop(0, NT // 4, body, jnp.zeros((8, TB), F32))

    class Scatter:
        def __init__(self, p, h):
            self.p = p = p * NH + h
            self.h = h
            top = spread(products(p))
            rate = (STEPS / top)[:1]
            unit[p] = top * (1.0 / STEPS)
            runit[p, j] = unit[p]
            zunit[p, z] = unit[p]
            self.rcopies, self.ccopies = [], []
            for d in (2, 3, 4, 5, 6, 7, 1):
                j_ = (y + d // 2) % 4 * 2 + (c + d) % 2
                self.rcopies.append(send(unit.at[p], runit.at[p, j], col_dev(xl, j_)))
            for d in (1, 3, 2):
                self.ccopies.append(send(unit.at[p], zunit.at[p, z], row_dev((z + d) % 4, xh)))

            def col_body(i, _):
                for x in range(2):
                    for q in range(GT):
                        scol[p, i, x, q] = code(chain[tab[LAST + (i * 2 + x) * GT + q]], rate)
                return 0

            lax.fori_loop(0, 4, col_body, 0)
            for d in (2, 1, 3):
                self.ccopies.append(
                    send(scol.at[p, (z + d) % 4], rcol.at[p, z], row_dev((z + d) % 4, xh))
                )

            def row_body(jj, _):
                for x in range(2):
                    for s in range(CAP):
                        srow[p, jj, x, s] = code(prod[tab[SLOT + (x * 8 + jj) * CAP + s]], rate)
                return 0

            lax.fori_loop(0, 8, row_body, 0)
            for d in (4, 5, 2, 3, 6, 7, 1):
                j_ = (y + d // 2) % 4 * 2 + (c + d) % 2
                self.rcopies.append(send(srow.at[p, j_], rrow.at[p, j], col_dev(xl, j_)))
            rcol[p, z] = scol[p, z]
            rrow[p, j] = srow[p, j]

        def middle(self):
            p, h = self.p, self.h
            for copy in self.ccopies:
                copy.wait_recv()

            def col_sum(x, q):
                total = plain(rcol[p, 0, x, q]) * zunit[p, 0, 0:1]
                for zz in range(1, 4):
                    total = total + plain(rcol[p, zz, x, q]) * zunit[p, zz, 0:1]
                return total

            def other_col(q, top):
                total = col_sum(oxh, q)
                acol[h, q] = total
                return jnp.maximum(top, largest(total))

            top = spread(lax.fori_loop(0, GT, other_col, jnp.zeros((8, TB), F32)))
            xhu[p] = top * (1.0 / STEPS)
            u2 = send(xhu.at[p], rxhu.at[p], row_dev(z, oxh))
            rate = (STEPS / top)[:1]

            def code_col(q, _):
                sxh[p, q] = code(acol[h, q], rate)
                return 0

            lax.fori_loop(0, GT, code_col, 0)
            s2 = send(sxh.at[p], rxh.at[p], row_dev(z, oxh))

            for copy in self.rcopies:
                copy.wait_recv()

            def row_sum(x):
                def chunk(kc, top):
                    rows = pl.ds(pl.multiple_of(kc * 16, 16), 16)

                    def source(jj, accs):
                        accs = list(accs)
                        factor = runit[p, jj]
                        for s in range(CAP):
                            data = plain(rrow[p, jj, x, s, rows]).reshape(2, 8, TB) * factor[None]
                            for q in range(GT):
                                accs[q] = accs[q] + data * mk[x, jj, s, q][None]
                        return tuple(accs)

                    accs = lax.fori_loop(
                        0, 8, source, tuple(jnp.zeros((2, 8, TB), F32) for _ in range(GT))
                    )
                    for q in range(GT):
                        value = accs[q].reshape(16, TB)
                        arow[h, q, rows] = value
                        top = jnp.maximum(top, largest(value))
                    return top

                return lax.fori_loop(0, KH // 16, chunk, jnp.zeros((8, TB), F32))

            top = spread(row_sum(oxl))
            xlu[p] = top * (1.0 / STEPS)
            u1 = send(xlu.at[p], rxlu.at[p], col_dev(oxl, j))
            rate = (STEPS / top)[:1]

            def code_row(q, _):
                sxl[p, q] = code(arow[h, q], rate)
                return 0

            lax.fori_loop(0, GT, code_row, 0)
            s1 = send(sxl.at[p], rxl.at[p], col_dev(oxl, j))
            row_sum(xl)

            def own_col(q, _):
                acol[h, q] = col_sum(xh, q)
                return 0

            lax.fori_loop(0, GT, own_col, 0)
            self.last = (u2, s2, u1, s1)

        def end(self):
            for copy in self.last:
                copy.wait_recv()

        def symmetric(self, q):
            p, h = self.p, self.h
            total = arow[h, q] + acol[h, q]
            total = total + plain(rxl[p, q]) * rxlu[p, 0:1] + plain(rxh[p, q]) * rxhu[p, 0:1]
            return 0.5 * total

    class Sum:
        def __init__(self, n, value):
            self.n = n
            sum_a[n, col] = jnp.concatenate([value[: K // 2], value[K // 2 :]], axis=1)
            self.copies = [
                send(sum_a.at[n, col], sum_a.at[n, col], (row, (col + d) % N_COL))
                for d in range(1, N_COL)
            ]

        def middle(self):
            n = self.n
            for copy in self.copies:
                copy.wait_recv()
            total = sum_a[n, 0]
            for r in range(1, N_COL):
                total = total + sum_a[n, r]
            sum_b[n, row] = total
            self.copies = [
                send(sum_b.at[n, row], sum_b.at[n, row], ((row + d) % N_ROW, col))
                for d in range(1, N_ROW)
            ]

        def end(self):
            n = self.n
            for copy in self.copies:
                copy.wait_recv()
            total = sum_b[n, 0]
            for r in range(1, N_ROW):
                total = total + sum_b[n, r]
            total = total * (1.0 / NN)
            return jnp.concatenate([total[:, :K], total[:, K:]], axis=0)

    prod[NT] = jnp.zeros((KH, TB), F32)
    chain[NT] = jnp.zeros((KH, TB), F32)
    load_v.wait()
    pl.semaphore_wait(barrier, N_ROW - 1 + N_COL - 1)
    gathers = [
        Gather(h, lambda q, h=h: v_ref[vecs(h), lanes(q)], h == 0) for h in range(NH)
    ]
    for h in range(NH):
        gathers[h].across()
        if h + 1 < NH:
            gathers[h + 1].near()
    load.wait()
    dcopies = degree_start()
    scatters = []
    for h in range(NH):
        gathers[h].relay()
        gathers[h].end()
        scatters.append(Scatter(0, h))
    dlast = degree_middle(dcopies)
    gathers = []
    for h in range(NH):
        s = scatters[h]
        s.middle()
        if h == 0:
            degree_end(dlast)
        else:
            gathers[h - 1].across()
        s.end()
        for q in range(GT):
            v = v_ref[vecs(h), lanes(q)]
            image = deg[q : q + 1] * v - s.symmetric(q)
            f1[vecs(h), lanes(q)] = (image - CENTER * v) / HALF_WIDTH
        gathers.append(Gather(NH + h, lambda q, h=h: f1[vecs(h), lanes(q)]))
    gathers[-1].across()
    scatters = []
    for h in range(NH):
        gathers[h].relay()
        gathers[h].end()
        scatters.append(Scatter(1, h))
    gathers = []
    for h in range(NH):
        s = scatters[h]
        s.middle()
        if h > 0:
            gathers[h - 1].across()
        s.end()
        for q in range(GT):
            v = f1[vecs(h), lanes(q)]
            image = deg[q : q + 1] * v - s.symmetric(q)
            f_ref[vecs(h), lanes(q)] = (
                2.0 * (image - CENTER * v) / HALF_WIDTH - v_ref[vecs(h), lanes(q)]
            )
        gathers.append(Gather(2 * NH + h, lambda q, h=h: f_ref[vecs(h), lanes(q)]))
    gram = jnp.zeros((K, K), F32)
    for q in range(GT):
        f = f_ref[:, lanes(q)]
        gram = gram + dot_t(f, f, precision=HIGH)
    gathers[-1].across()
    gsum = Sum(0, gram)
    diag = jnp.zeros((K, K), F32)
    for q in range(GT):
        f = f_ref[:, lanes(q)]
        diag = diag + dot_t(f, deg[q : q + 1] * f, precision=HIGH)
    for g in gathers:
        g.relay()
    for g in gathers:
        g.end()
    gsum.middle()

    def form(i, acc):
        parts = []
        for u in range(4):
            t = i * 4 + u
            left = jnp.concatenate([colp[2 * NH + h][tab[COLS + t]] for h in range(NH)], axis=0)
            parts.append(dot_t(left, tiles[t]).astype(BF16))
        for u in range(4):
            t = i * 4 + u
            right = jnp.concatenate([rowp[2 * NH + h][tab[ROWS + t]] for h in range(NH)], axis=0)
            acc = acc + dot_t(parts[u], right)
        return acc

    form_w = lax.fori_loop(0, NT // 4, form, jnp.zeros((K, K), F32))
    qsum = Sum(1, diag - form_w)
    gram = gsum.end()
    sub = lax.broadcasted_iota(jnp.int32, (K, 2 * K), 0)
    lane = lax.broadcasted_iota(jnp.int32, (K, 2 * K), 1)
    eye = jnp.where(lane == sub + K, 1.0, 0.0)
    a = jnp.where(lane < K, jnp.concatenate([gram, gram], axis=1), eye)

    def eliminate(a, steps):
        for i in steps:
            square = a[i : i + 1, i : i + 1]
            inv = lax.rsqrt(square)
            inv = inv * (1.5 - 0.5 * square * inv * inv)
            pivot = a[i : i + 1] * inv
            column = jnp.where(sub[:, :1] > i, a[:, i : i + 1] * inv, 0.0)
            a = jnp.where(sub == i, pivot, a - column * pivot)
        return a

    a = eliminate(a, range(K // 2))
    qsum.middle()
    a = eliminate(a, range(K // 2, K))
    inverse = a[:, K:]
    q = qsum.end()
    half = dot_n(inverse, q, precision=HIGH)
    ray = 0.5 * (dot_t(half, inverse, precision=HIGH) + dot_t(inverse, half, precision=HIGH))
    ray_ref[...] = ray
    ritz_ref[...] = dot_n(dot_n(ray, inverse, precision=HIGH), f_ref[...], precision=HIGH)
    for copy in sent:
        copy.wait_send()


def local(tiles, tile_rows, tile_cols, start_vectors):
    smem = pl.BlockSpec(memory_space=pltpu.SMEM)
    vmem = pl.BlockSpec(memory_space=pltpu.VMEM)
    table = pl.pallas_call(
        table_kernel,
        out_shape=jax.ShapeDtypeStruct((TAB,), jnp.int32),
        in_specs=[smem, smem],
        out_specs=smem,
        scratch_shapes=[pltpu.SMEM((N_COL,), jnp.int32)],
    )(tile_rows.reshape(NT), tile_cols.reshape(NT))
    own = start_vectors.shape[1]
    V = pltpu.VMEM
    RH = 2 * NH
    return pl.pallas_call(
        main_kernel,
        out_shape=(
            jax.ShapeDtypeStruct((K, own), F32),
            jax.ShapeDtypeStruct((K, K), F32),
        ),
        in_specs=[smem, pl.BlockSpec(memory_space=pl.ANY), pl.BlockSpec(memory_space=pl.ANY)],
        out_specs=(vmem, vmem),
        scratch_shapes=[
            V((NT, TB, TB), BF16), V((K, own), F32), [V((64, KH, TB), BF16)] * PH, [V((128, KH, TB), BF16)] * PH,
            V((NT + 1, KH, TB), F32), V((NT + 1, KH, TB), F32),
            V((RH, 8, 2, CAP, KH, TB), I16), V((RH, 8, 2, CAP, KH, TB), I16),
            V((RH, 4, 2, GT, KH, TB), I16), V((RH, 4, 2, GT, KH, TB), I16),
            V((RH, GT, KH, TB), I16), V((RH, GT, KH, TB), I16),
            V((RH, GT, KH, TB), I16), V((RH, GT, KH, TB), I16),
            V((NH, GT, KH, TB), F32), V((NH, GT, KH, TB), F32),
            V((NT + 1, 8, TB), F32), V((NT + 1, 8, TB), F32),
            V((8, 16, TB), F32), V((8, 16, TB), F32),
            V((4, 16, TB), F32), V((4, 16, TB), F32),
            V((8, TB), F32), V((8, TB), F32), V((8, TB), F32), V((8, TB), F32),
            V((8, TB), F32), V((2, 8, CAP, GT, 8, TB), F32), V((K, own), F32), V((K, own), F32),
            V((2, 16, K // 2, TB), F32), V((2, 8, K // 2, TB), F32),
            V((RH, 8, TB), F32), V((RH, 8, 8, TB), F32), V((RH, 4, 8, TB), F32),
            V((RH, 8, TB), F32), V((RH, 8, TB), F32), V((RH, 8, TB), F32), V((RH, 8, TB), F32),
            pltpu.SemaphoreType.DMA((NSEM,)), pltpu.SemaphoreType.DMA((NSEM,)),
            pltpu.SemaphoreType.DMA((2,)),
        ],
        compiler_params=pltpu.CompilerParams(
            collective_id=0, has_side_effects=True, vmem_limit_bytes=67_043_328
        ),
    )(table, tiles.reshape(NT, TB, TB), start_vectors)


def solution(mesh):
    placed = (
        P("row", "col", None, None, None),
        P("row", "col", None),
        P("row", "col", None),
        P(None, ("row", "col")),
    )
    return jax.shard_map(
        local, mesh=mesh, in_specs=placed, out_specs=(P(None, ("row", "col")), P()), check_vma=False
    )
```
